512 devices in a mesh: grp: 16 (over z, core), sub: 32 (over y, x).
Axes of the slice: x: 4, y: 8, z: 8, core: 2. Of those that a mesh axis runs over, the one named last changes fastest.
Arguments:
- right_side: float32 [8192, 512], P(('grp', 'sub')), may hold values from -8 to 8
- metric: float32 [8192, 1536], P(('grp', 'sub')), may hold values from 0.3 to 3
- helmholtz: float32 [8192, 512], P(('grp', 'sub')), may hold values from 0.5 to 2
- jacobi: float32 [8192, 512], P(('grp', 'sub')), may hold values from 0.05 to 0.5
- pair_list: int32 [2, 524288], P(None, ('grp', 'sub')), may hold values from 0 to 8191
- shared_slots: int32 [512, 32, 128], P(('grp', 'sub')), may hold values from 0 to 8192, as said below
- face_points: int32 [2, 262144], P(None, ('grp', 'sub')), may hold values from 0 to 8191
- coarse_map: int32 [8, 8192], P(None, ('grp', 'sub')), may hold values from 0 to 63
- coarse_inverse: float32 [16, 64, 64], P('grp'), as said below
Outputs:
- solution: float32 [8192, 512], P(('grp', 'sub'))
- residual: float32 [8192, 512], P(('grp', 'sub'))
The draws below stay inside these ranges and needn't reach their ends.
Inputs may be any that keep to these rules, and one draw needn't show every extreme that they name: `shared_slots`: entries equal to 8192 mark empty slots; the slot of device a for peer b in one group is filled exactly when the slot of b for a at the same position is; a device's slots for itself are empty; filled slots come first in each row. `coarse_inverse`: each group's matrix is symmetric and positive definite.
All inputs are finite; a program needn't handle non-finite values.
Results may differ from the reference program's by a relative error of at most 0.0003.
Values sent between devices are 32-bit elements; how exact they have to be, the bound alone decides.
A program may use at most 64 MiB of HBM per device.

```python
import math
import jax
import jax.numpy as jnp
import numpy as np
from jax import lax

POINTS = 512
E_DEV = 16
CAP = 128
ITERS = 2
LP = 1024
FC = 512
NC = 64
ELEMENTS = 8192
N_GRP = 16
N_SUB = 32
DEVICES = 512


def draw_shared_slots(key, part):
    key_near, key_count, key_index = jax.random.split(key, 3)
    first_peer = jnp.arange(N_SUB, dtype=jnp.int32)[None, :, None]
    second_peer = jnp.arange(N_SUB, dtype=jnp.int32)[None, None, :]
    upper = first_peer < second_peer
    near = (jax.random.randint(key_near, (N_GRP, N_SUB, N_SUB), 0, 10) < 7).astype(jnp.int32)
    counts = jax.random.randint(key_count, (N_GRP, N_SUB, N_SUB), 3 * CAP // 8, CAP + 1)
    near = jnp.where(upper, near, jnp.swapaxes(near, 1, 2))
    counts = jnp.where(upper, counts, jnp.swapaxes(counts, 1, 2))
    pinned = (first_peer == 0) & (second_peer == 1) | (first_peer == 1) & (second_peer == 0)
    counts = jnp.where(pinned, CAP, jnp.where(near == 1, counts, 0))
    counts = jnp.where(first_peer == second_peer, 0, counts)
    indices = jax.random.randint(key_index, (N_GRP, N_SUB, N_SUB, CAP), 0, E_DEV * 512)
    position = jnp.arange(CAP, dtype=jnp.int32)[None, None, None, :]
    filled = position < counts[:, :, :, None]
    slots = jnp.where(filled, indices, E_DEV * 512)
    return slots.reshape(N_GRP * N_SUB, N_SUB, CAP).astype(jnp.int32)


def draw_coarse_inverse(key, part):
    key_off, key_diag = jax.random.split(key, 2)
    mixed = jax.random.uniform(key_off, (N_GRP, NC, NC), jnp.float32, -1.0, 1.0)
    symmetric = 0.5 * (mixed + jnp.swapaxes(mixed, 1, 2))
    diagonal = jax.random.uniform(key_diag, (N_GRP, NC), jnp.float32, 0.002, 0.004)
    row_index = jnp.arange(NC)[:, None]
    column_index = jnp.arange(NC)[None, :]
    result = jnp.where((row_index == column_index)[None, :, :], diagonal[:, :, None], 0.002 * symmetric / NC)
    return result.astype(jnp.float32)


def with_ends(array, key, low, largest):
    shape = array.shape
    index_at = [jax.random.randint(jax.random.fold_in(key, axis), (), 0, shape[axis]) for axis in range(len(shape))]
    array = array.at[tuple(index_at)].set(low)
    longest = shape.index(max(shape))
    index_at[longest] = (index_at[longest] + 1) % shape[longest]
    return array.at[tuple(index_at)].set(largest)


def shard_levels(own_key, shape, shards, smallest, high):
    def one(dim, parts):
        heights = jax.random.uniform(jax.random.fold_in(jax.random.fold_in(own_key, 6), dim), (parts,), jnp.float32, smallest / len(shards), high / len(shards))
        return jnp.repeat(jnp.exp(heights), shape[dim] // parts).reshape((-1,) + (1,) * (len(shape) - dim - 1))

    level = one(*shards[0])
    for cut in shards[1:]:
        level = level * one(*cut)
    return level


def gaussian(stream_key, dims, scale, reach, shards=(), kind=jnp.bfloat16):
    gain = shard_levels(stream_key, dims, shards, -0.22, 0.18) if shards else 1.0
    array = jax.random.normal(stream_key, dims, jnp.float32) * scale * gain
    return jnp.minimum(jnp.maximum(array, -reach), reach).astype(kind)


def setup_inputs(seed: int = 0) -> dict:
    seeds = jax.random.split(jax.random.key(seed), 10)
    return {
        "right_side": gaussian(seeds[0], (ELEMENTS, POINTS), 1.0, 8.0, ((0, 512),), jnp.float32),
        "metric": jnp.clip(jnp.exp(math.log(3.0) - 2.3025851 * jax.random.uniform(seeds[1], (ELEMENTS, 3 * POINTS), jnp.float32) ** shard_levels(seeds[1], (ELEMENTS, 3 * POINTS), ((0, 512),), -0.2, 0.2)), 0.3, 3.0),
        "helmholtz": jnp.clip(jnp.exp(math.log(2.0) - 1.3862944 * jax.random.uniform(seeds[2], (ELEMENTS, POINTS), jnp.float32) ** shard_levels(seeds[2], (ELEMENTS, POINTS), ((0, 512),), -0.2, 0.2)), 0.5, 2.0),
        "jacobi": jnp.clip(jnp.exp(math.log(0.5) - 2.3025851 * jax.random.uniform(seeds[3], (ELEMENTS, POINTS), jnp.float32) ** shard_levels(seeds[3], (ELEMENTS, POINTS), ((0, 512),), -0.2, 0.2)), 0.05, 0.5),
        "pair_list": with_ends(jax.random.randint(seeds[4], (2, LP * DEVICES), 0, E_DEV * 512), jax.random.fold_in(seeds[4], 1), 0, (E_DEV * 512) - 1).astype(jnp.int32),
        "shared_slots": draw_shared_slots(jax.random.fold_in(seeds[9], 71), 0),
        "face_points": with_ends(jax.random.randint(seeds[6], (2, FC * DEVICES), 0, E_DEV * 512), jax.random.fold_in(seeds[6], 1), 0, (E_DEV * 512) - 1).astype(jnp.int32),
        "coarse_map": with_ends(jax.random.randint(seeds[7], (8, ELEMENTS), 0, NC), jax.random.fold_in(seeds[7], 1), 0, NC - 1).astype(jnp.int32),
        "coarse_inverse": draw_coarse_inverse(jax.random.fold_in(seeds[9], 71), 0),
    }


def tables():
    order_index = np.arange(8)
    colloc = np.cos(np.pi * order_index / 7.0)
    end_weights = np.where((order_index == 0) | (order_index == 7), 2.0, 1.0) * (-1.0) ** order_index
    spacing = colloc[:, None] - colloc[None, :] + np.eye(8)
    raw_matrix = np.outer(end_weights, 1.0 / end_weights) / spacing
    off_part = raw_matrix * (1.0 - np.eye(8))
    derivative = 0.25 * (off_part - np.eye(8) * off_part.sum(axis=1)[:, None])
    point_index = np.arange(512)
    corner_index = np.arange(8)
    sign_first = 1.0 - 2.0 * ((corner_index >> 2) & 1)
    sign_second = 1.0 - 2.0 * ((corner_index >> 1) & 1)
    sign_third = 1.0 - 2.0 * (corner_index & 1)
    node_first = colloc[point_index // 64][:, None]
    node_second = colloc[(point_index // 8) % 8][:, None]
    node_third = colloc[point_index % 8][:, None]
    corner = (0.5 * (1.0 + sign_first[None, :] * node_first)) * (0.5 * (1.0 + sign_second[None, :] * node_second)) * (0.5 * (1.0 + sign_third[None, :] * node_third))
    return jnp.asarray(derivative, jnp.float32), jnp.asarray(corner, jnp.float32)


def reference(right_side, metric, helmholtz, jacobi, pair_list, shared_slots, face_points, coarse_map, coarse_inverse):
    derivative, corner = tables()
    highest = lax.Precision.HIGHEST
    points = E_DEV * 512
    devices_all = N_GRP * N_SUB

    def assemble(field):
        flat = field.reshape(-1)
        owner = jnp.arange(devices_all * LP, dtype=jnp.int32) // LP
        first = owner * points + pair_list[0]
        second = owner * points + pair_list[1]
        total = flat.at[first].add(flat[second]).at[second].add(flat[first])
        by_device = field.reshape(devices_all, points)
        padded = jnp.concatenate([by_device, jnp.zeros((devices_all, 1), jnp.float32)], axis=1)
        slots = shared_slots.reshape(devices_all, N_SUB * CAP)
        sent = jnp.take_along_axis(padded, slots, axis=1).reshape(N_GRP, N_SUB, N_SUB, CAP)
        received = jnp.swapaxes(sent, 1, 2).reshape(devices_all, N_SUB * CAP)
        row_base = (jnp.arange(devices_all, dtype=jnp.int32) * (points + 1))[:, None]
        spread = jnp.zeros((devices_all * (points + 1),), jnp.float32)
        spread = spread.at[(row_base + slots).reshape(-1)].add(received.reshape(-1))
        total = total + spread.reshape(devices_all, points + 1)[:, :points].reshape(-1)
        faces = face_points.reshape(2, devices_all, FC)
        values_down = jnp.take_along_axis(by_device, faces[0], axis=1).reshape(N_GRP, N_SUB, FC)
        values_up = jnp.take_along_axis(by_device, faces[1], axis=1).reshape(N_GRP, N_SUB, FC)
        zero_row = jnp.zeros((1, N_SUB, FC), jnp.float32)
        into_down = jnp.concatenate([zero_row, values_up[:-1]], axis=0).reshape(-1)
        into_up = jnp.concatenate([values_down[1:], zero_row], axis=0).reshape(-1)
        base = (jnp.arange(devices_all, dtype=jnp.int32) * points)[:, None]
        total = total.at[(base + faces[0]).reshape(-1)].add(into_down)
        total = total.at[(base + faces[1]).reshape(-1)].add(into_up)
        return total.reshape(field.shape)

    def stiffness(field):
        cube = field.reshape(-1, 8, 8, 8)
        grad_first = jnp.einsum('ai,eijk->eajk', derivative, cube, precision=highest)
        grad_second = jnp.einsum('bj,eijk->eibk', derivative, cube, precision=highest)
        grad_third = jnp.einsum('ck,eijk->eijc', derivative, cube, precision=highest)
        flux_first = metric[:, :512].reshape(-1, 8, 8, 8) * grad_first
        flux_second = metric[:, 512:1024].reshape(-1, 8, 8, 8) * grad_second
        flux_third = metric[:, 1024:].reshape(-1, 8, 8, 8) * grad_third
        back = jnp.einsum('ai,eajk->eijk', derivative, flux_first, precision=highest)
        back = back + jnp.einsum('bj,eibk->eijk', derivative, flux_second, precision=highest)
        back = back + jnp.einsum('ck,eijc->eijk', derivative, flux_third, precision=highest)
        return back.reshape(-1, 512)

    def operate(field):
        return assemble(stiffness(assemble(field))) + helmholtz * field

    group_of = jnp.arange(ELEMENTS, dtype=jnp.int32) // (E_DEV * N_SUB)
    vertex_ids = group_of[:, None] * NC + coarse_map.T

    def precondition(resid):
        vertex = jnp.dot(resid, corner, precision=highest)
        coarse = jax.ops.segment_sum(vertex.reshape(-1), vertex_ids.reshape(-1), num_segments=N_GRP * NC).reshape(N_GRP, NC)
        solved = jnp.einsum('gij,gj->gi', coarse_inverse, coarse, precision=highest)
        at_vertex = solved.reshape(-1)[vertex_ids]
        return jacobi * resid + jnp.dot(at_vertex, corner.T, precision=highest)

    solution = jnp.zeros_like(right_side)
    residual = right_side
    smoothed = precondition(residual)
    direction = smoothed
    rz_now = jnp.sum(residual * smoothed)
    for iteration in range(ITERS):
        image = operate(direction)
        alpha = rz_now / jnp.sum(direction * image)
        solution = solution + alpha * direction
        residual = residual - alpha * image
        if iteration + 1 < ITERS:
            smoothed = precondition(residual)
            rz_new = jnp.sum(residual * smoothed)
            direction = smoothed + (rz_new / rz_now) * direction
            rz_now = rz_new
    return solution, residual
```

```python
import functools

import jax
import jax.numpy as jnp
import numpy as np
from jax import lax
from jax.experimental import pallas as pl
from jax.experimental.pallas import tpu as pltpu
from jax.sharding import PartitionSpec as P

MESH = pl.DeviceIdType.MESH
F32 = jnp.float32
BF16 = jnp.bfloat16
PAIR = 8
FACE = 4


def tables():
    order_index = np.arange(8)
    colloc = np.cos(np.pi * order_index / 7.0)
    end_weights = (
        np.where((order_index == 0) | (order_index == 7), 2.0, 1.0) * (-1.0) ** order_index
    )
    spacing = colloc[:, None] - colloc[None, :] + np.eye(8)
    raw_matrix = np.outer(end_weights, 1.0 / end_weights) / spacing
    off_part = raw_matrix * (1.0 - np.eye(8))
    derivative = 0.25 * (off_part - np.eye(8) * off_part.sum(axis=1)[:, None])
    derivative = derivative.astype(np.float32).astype(np.float64)
    eye2, eye8, eye16 = np.eye(2), np.eye(8), np.eye(16)

    def rows_matrix(mat):
        def part(out_low, in_low):
            return np.kron(mat[out_low::2, in_low::2], eye16)

        return np.block([[part(0, 0), part(0, 1)], [part(1, 1), part(1, 0)]])

    along_second = np.kron(eye2, np.kron(derivative, eye8)).T
    along_third = np.kron(eye16, derivative).T
    stack = [
        along_second,
        along_third,
        along_second.T,
        along_third.T,
        rows_matrix(derivative),
        rows_matrix(derivative.T),
    ]
    high = [np.asarray(m, np.float32).astype(jnp.bfloat16) for m in stack]
    low = [
        (np.asarray(m, np.float32) - h.astype(np.float32)).astype(jnp.bfloat16)
        for m, h in zip(stack, high)
    ]
    mats = np.stack(high + low)
    point_index = np.arange(512)
    corner_index = np.arange(8)
    sign_first = 1.0 - 2.0 * (corner_index >> 2 & 1)
    sign_second = 1.0 - 2.0 * (corner_index >> 1 & 1)
    sign_third = 1.0 - 2.0 * (corner_index & 1)
    node_first = colloc[point_index // 64][:, None]
    node_second = colloc[point_index // 8 % 8][:, None]
    node_third = colloc[point_index % 8][:, None]
    corner = (
        0.5
        * (1.0 + sign_first[None, :] * node_first)
        * (0.5 * (1.0 + sign_second[None, :] * node_second))
        * (0.5 * (1.0 + sign_third[None, :] * node_third))
    )
    return jnp.asarray(mats), jnp.asarray(corner.T, F32)


def kernel(
    ns,
    ng,
    right_ref,
    metric_ref,
    helm_ref,
    jac_ref,
    pair_ref,
    slots_ref,
    face_ref,
    map_ref,
    cinv_ref,
    mats_ref,
    corner_ref,
    sol_ref,
    res_ref,
    idx,
    hi_ref,
    lo_ref,
    ohlo,
    x_ref,
    val_ref,
    cscr,
    mcol,
    send_s,
    recv_s,
    send_f,
    recv_f,
    send_r,
    recv_r,
    send_b,
    recv_b,
    send_sem,
    recv_sem,
):
    g = lax.axis_index("grp")
    s = lax.axis_index("sub")
    nxt, prv = lax.rem(g + 1, ng), lax.rem(g + ng - 1, ng)
    rows = 2 * PAIR + ns + 2 * FACE
    tiles = rows // 8
    at_face = 2 * PAIR + ns

    recv_s[...] = jnp.zeros_like(recv_s)

    barrier = pltpu.get_barrier_semaphore()

    def greet_sub(k, carry):
        pl.semaphore_signal(
            barrier, inc=1, device_id={"sub": lax.rem(s + k, ns)}, device_id_type=MESH
        )
        return carry

    def greet_grp(k, carry):
        pl.semaphore_signal(
            barrier, inc=1, device_id={"grp": lax.rem(g + k, ng)}, device_id_type=MESH
        )
        return carry

    lax.fori_loop(1, ns, greet_sub, 0)
    lax.fori_loop(1, ng, greet_grp, 0)

    def cube(ref, base=0):
        return jnp.concatenate(
            [ref[:, base + 128 * k : base + 128 * (k + 1)] for k in range(4)], axis=0
        )

    def total(x):
        return jnp.sum(jnp.sum(x, axis=0, keepdims=True), axis=1, keepdims=True)

    lane = lax.broadcasted_iota(jnp.int32, (1, 128), 1)

    def pick(row, k):
        return jnp.sum(jnp.where(lane == k, row, 0.0), axis=1, keepdims=True)

    def put(k, value):
        return jnp.where(lane == k, value, 0.0)

    eye_16 = lax.broadcasted_iota(jnp.int32, (16, 16), 0) == lax.broadcasted_iota(
        jnp.int32, (16, 16), 1
    )
    lane_16 = lax.broadcasted_iota(jnp.int32, (16, 128), 1).astype(F32)
    for q in range(8):
        column = jnp.sum(
            jnp.where(eye_16, map_ref[q : q + 1, :].astype(F32), 0.0), axis=1, keepdims=True
        )
        mcol[q] = jnp.where(lane_16 == column, 1.0, 0.0)
    cscr[...] = jnp.zeros_like(cscr)
    cscr[:, :64] = cinv_ref[0]

    def restrict(x):
        row = jnp.zeros((1, 128), F32)
        for q in range(8):
            acc = x[:16] * corner_ref[q : q + 1, :128]
            for k in range(1, 4):
                acc += x[16 * k : 16 * (k + 1)] * corner_ref[q : q + 1, 128 * k : 128 * (k + 1)]
            vertex = jnp.sum(acc, axis=1, keepdims=True)
            row += jnp.sum(vertex * mcol[q], axis=0, keepdims=True)
        return row

    eye_64 = lax.broadcasted_iota(jnp.int32, (64, 128), 0) == lax.broadcasted_iota(
        jnp.int32, (64, 128), 1
    )

    def prolong(coarse):
        column = jnp.sum(jnp.where(eye_64, coarse, 0.0), axis=1, keepdims=True)
        solved = jnp.sum(cscr[...] * column, axis=0, keepdims=True)
        blocks = [jnp.zeros((16, 128), F32) for _ in range(4)]
        for q in range(8):
            at_vertex = jnp.sum(mcol[q] * solved, axis=1, keepdims=True)
            for k in range(4):
                blocks[k] += at_vertex * corner_ref[q : q + 1, 128 * k : 128 * (k + 1)]
        return jnp.concatenate(blocks, axis=0)

    def copy_sub(src, dst, sem, peer):
        return pltpu.make_async_remote_copy(
            src_ref=src,
            dst_ref=dst,
            send_sem=send_sem.at[sem],
            recv_sem=recv_sem.at[sem],
            device_id={"sub": peer},
            device_id_type=MESH,
        )

    def copy_grp(src, dst, sem, peer):
        return pltpu.make_async_remote_copy(
            src_ref=src,
            dst_ref=dst,
            send_sem=send_sem.at[sem],
            recv_sem=recv_sem.at[sem],
            device_id={"grp": peer},
            device_id_type=MESH,
        )

    def wait_bytes(ref, sem):
        pltpu.make_async_copy(ref, ref, sem).wait()

    def reduce_sub(phase, row):
        send_r[phase] = row
        recv_r[phase, s] = row

        def go(k, carry):
            peer = lax.rem(s + k, ns)
            copy_sub(send_r.at[phase], recv_r.at[phase, s], 12 + phase, peer).start()
            return carry

        lax.fori_loop(1, ns, go, 0)
        wait_bytes(recv_r.at[phase, pl.ds(0, ns - 1)], recv_sem.at[12 + phase])
        return jnp.sum(recv_r[phase], axis=0)

    def reduce_grp(phase, row):
        send_b[phase] = row
        recv_b[phase, g] = row

        def go(k, carry):
            peer = lax.rem(g + k, ng)
            copy_grp(send_b.at[phase], recv_b.at[phase, g], 15 + phase, peer).start()
            return carry

        lax.fori_loop(1, ng, go, 0)
        wait_bytes(recv_b.at[phase, pl.ds(0, ng - 1)], recv_sem.at[15 + phase])
        return jnp.sum(recv_b[phase], axis=0)

    residual = cube(right_ref)
    partial_coarse = restrict(residual)

    for k in range(PAIR):
        idx[k : k + 1, :] = pair_ref[0:1, 128 * k : 128 * (k + 1)]
        idx[PAIR + k : PAIR + k + 1, :] = pair_ref[1:2, 128 * k : 128 * (k + 1)]
    idx[2 * PAIR : at_face, :] = slots_ref[0]
    for k in range(FACE):
        idx[at_face + k : at_face + k + 1, :] = face_ref[0:1, 128 * k : 128 * (k + 1)]
        idx[at_face + FACE + k : at_face + FACE + k + 1, :] = face_ref[
            1:2, 128 * k : 128 * (k + 1)
        ]
    points = idx[...]
    row_of = ((points >> 7) & 3) * 16 + (points >> 9)
    hi_ref[...] = jnp.where(points >= 8192, 1024, row_of)
    lo_ref[...] = points & 127

    pl.semaphore_wait(barrier, ns + ng - 2)

    coarse = reduce_sub(0, partial_coarse)

    sub_128 = lax.broadcasted_iota(jnp.int32, (128, 128), 0)
    sub_64 = lax.broadcasted_iota(jnp.int32, (64, 128), 0)

    def build(t, carry):
        low = lo_ref[pl.ds(pl.multiple_of(t * 8, 8), 8), :]
        ohlo[t] = jnp.concatenate(
            [jnp.where(sub_128 == low[r : r + 1], 1.0, 0.0).astype(BF16) for r in range(8)],
            axis=1,
        )
        return carry

    lax.fori_loop(0, tiles, build, 0)

    def gather(x):
        x_ref[...] = x
        high = hi_ref[...]
        low = lo_ref[...]

        def step(t, acc):
            block = x_ref[pl.ds(pl.multiple_of(t * 8, 8), 8), :]
            for r in range(8):
                row = jnp.broadcast_to(block[r : r + 1], (rows, 128))
                got = jnp.take_along_axis(row, low, axis=1, mode="promise_in_bounds")
                acc = jnp.where(high == t * 8 + r, got, acc)
            return acc

        return lax.fori_loop(0, 8, step, jnp.zeros((rows, 128), F32))

    def scatter(first, last, acc):
        def step(t, acc):
            at = pl.ds(pl.multiple_of(t * 8, 8), 8)
            high = hi_ref[at, :]
            value = val_ref[at, :]
            upper = value.astype(BF16).astype(F32)
            lower = value - upper
            parts = []
            for r in range(8):
                hit = sub_64 == high[r : r + 1]
                parts.append(
                    jnp.concatenate(
                        [
                            jnp.where(hit, upper[r : r + 1], 0.0),
                            jnp.where(hit, lower[r : r + 1], 0.0),
                        ],
                        axis=0,
                    ).astype(BF16)
                )
            left = jnp.concatenate(parts, axis=1)
            return acc + lax.dot_general(
                left, ohlo[t], (((1,), (1,)), ((), ())), preferred_element_type=F32
            )

        return lax.fori_loop(first, last, step, acc)

    def assemble(phase, x):
        got = gather(x)
        send_s[phase] = got[2 * PAIR : at_face].reshape(ns, 1, 128)
        send_f[phase, 0] = got[at_face : at_face + FACE]
        send_f[phase, 1] = got[at_face + FACE :]

        def go(k, carry):
            peer = lax.rem(s + k, ns)
            copy_sub(send_s.at[phase, peer], recv_s.at[phase, s], phase, peer).start()
            return carry

        lax.fori_loop(1, ns, go, 0)
        down = copy_grp(send_f.at[phase, 0], recv_f.at[phase, 1], 4 + phase, prv)
        up = copy_grp(send_f.at[phase, 1], recv_f.at[phase, 0], 8 + phase, nxt)
        down.start()
        up.start()
        val_ref[0:PAIR, :] = got[PAIR : 2 * PAIR]
        val_ref[PAIR : 2 * PAIR, :] = got[0:PAIR]
        acc = scatter(0, 2, jnp.zeros((128, 128), F32))
        down.wait_recv()
        up.wait_recv()
        val_ref[at_face : at_face + FACE, :] = jnp.where(g == 0, 0.0, recv_f[phase, 0])
        val_ref[at_face + FACE :, :] = jnp.where(g == ng - 1, 0.0, recv_f[phase, 1])
        acc = scatter(tiles - 1, tiles, acc)
        wait_bytes(recv_s.at[phase, pl.ds(0, ns - 1)], recv_sem.at[phase])
        val_ref[2 * PAIR : at_face, :] = recv_s[phase].reshape(ns, 128)
        acc = scatter(2, tiles - 1, acc)
        return x + acc[:64] + acc[64:]

    def split(x):
        upper = x.astype(BF16)
        return upper, (x - upper.astype(F32)).astype(BF16)

    def dot(a, b):
        return jnp.dot(a, b, preferred_element_type=F32)

    def dot_right(x, k):
        upper, lower = split(x)
        both = dot(jnp.concatenate([upper, lower], axis=0), mats_ref[k])
        return both[:64] + both[64:] + dot(upper, mats_ref[k + 6])

    left_half = lax.broadcasted_iota(jnp.int32, (64, 128), 1) < 64

    def dot_rows(x, k):
        upper, lower = split(jnp.concatenate([x, pltpu.roll(x, 64, 1)], axis=0))
        both = dot(mats_ref[k], jnp.concatenate([upper, lower], axis=1))
        out = both[:, :128] + both[:, 128:] + dot(mats_ref[k + 6], upper)
        return jnp.where(left_half, out[:64], out[64:])

    def stiffness(x):
        flux_first = cube(metric_ref, 0) * dot_rows(x, 4)
        flux_second = cube(metric_ref, 512) * dot_right(x, 0)
        flux_third = cube(metric_ref, 1024) * dot_right(x, 1)
        return dot_rows(flux_first, 5) + dot_right(flux_second, 2) + dot_right(flux_third, 3)

    def operate(phase, x):
        summed = assemble(phase, x)
        return assemble(phase + 1, stiffness(summed)) + cube(helm_ref) * x

    direction = cube(jac_ref) * residual + prolong(coarse)
    rz_local = total(residual * direction)
    image = operate(0, direction)
    row = restrict(image) + put(64, rz_local) + put(65, total(direction * image))
    row = reduce_sub(1, row)
    sums = reduce_grp(0, row)
    rz_first, curved = pick(sums, 64), pick(sums, 65)
    alpha = rz_first / curved
    residual = residual - alpha * image
    coarse = coarse - alpha * row
    smoothed = cube(jac_ref) * residual + prolong(coarse)
    operated = operate(2, smoothed)
    row = (
        put(64, total(residual * smoothed))
        + put(65, total(smoothed * operated))
        + put(66, total(smoothed * image + direction * operated))
    )
    sums = reduce_grp(1, reduce_sub(2, row))
    rz_second = pick(sums, 64)
    beta = rz_second / rz_first
    curve = pick(sums, 65) + beta * pick(sums, 66) + beta * beta * curved
    alpha_last = rz_second / curve
    solved = alpha * direction + alpha_last * (smoothed + beta * direction)
    residual = residual - alpha_last * (operated + beta * image)
    for k in range(4):
        sol_ref[:, 128 * k : 128 * (k + 1)] = solved[16 * k : 16 * (k + 1)]
        res_ref[:, 128 * k : 128 * (k + 1)] = residual[16 * k : 16 * (k + 1)]

    for phase in range(4):
        wait_bytes(send_s.at[phase, pl.ds(0, ns - 1)], send_sem.at[phase])
        wait_bytes(send_f.at[phase, 0], send_sem.at[4 + phase])
        wait_bytes(send_f.at[phase, 1], send_sem.at[8 + phase])
    for phase in range(3):
        wait_bytes(recv_r.at[phase, pl.ds(0, ns - 1)], send_sem.at[12 + phase])
    for phase in range(2):
        wait_bytes(recv_b.at[phase, pl.ds(0, ng - 1)], send_sem.at[15 + phase])


def body(ns, ng, *args):
    mats, corner = tables()
    rows = 2 * PAIR + ns + 2 * FACE
    vmem = pl.BlockSpec(memory_space=pltpu.VMEM)
    shape = jax.ShapeDtypeStruct((16, 512), F32)
    return pl.pallas_call(
        functools.partial(kernel, ns, ng),
        out_shape=(shape, shape),
        in_specs=[vmem] * 11,
        out_specs=(vmem, vmem),
        scratch_shapes=[
            pltpu.VMEM((rows, 128), jnp.int32),
            pltpu.VMEM((rows, 128), jnp.int32),
            pltpu.VMEM((rows, 128), jnp.int32),
            pltpu.VMEM((rows // 8, 128, 1024), BF16),
            pltpu.VMEM((64, 128), F32),
            pltpu.VMEM((rows, 128), F32),
            pltpu.VMEM((64, 128), F32),
            pltpu.VMEM((8, 16, 128), F32),
            pltpu.VMEM((4, ns, 1, 128), F32),
            pltpu.VMEM((4, ns, 1, 128), F32),
            pltpu.VMEM((4, 2, FACE, 128), F32),
            pltpu.VMEM((4, 2, FACE, 128), F32),
            pltpu.VMEM((3, 1, 128), F32),
            pltpu.VMEM((3, ns, 1, 128), F32),
            pltpu.VMEM((2, 1, 128), F32),
            pltpu.VMEM((2, ng, 1, 128), F32),
            pltpu.SemaphoreType.DMA((17,)),
            pltpu.SemaphoreType.DMA((17,)),
        ],
        compiler_params=pltpu.CompilerParams(collective_id=0, has_side_effects=True),
    )(*args, mats, corner)


def solution(mesh):
    in_specs = (
        P(("grp", "sub"), None),
        P(("grp", "sub"), None),
        P(("grp", "sub"), None),
        P(("grp", "sub"), None),
        P(None, ("grp", "sub")),
        P(("grp", "sub"), None, None),
        P(None, ("grp", "sub")),
        P(None, ("grp", "sub")),
        P("grp", None, None),
    )
    out_specs = (P(("grp", "sub"), None), P(("grp", "sub"), None))
    return jax.shard_map(
        functools.partial(body, mesh.shape["sub"], mesh.shape["grp"]),
        mesh=mesh,
        in_specs=in_specs,
        out_specs=out_specs,
        check_vma=False,
    )
```

```python
import functools

import jax
import jax.numpy as jnp
import numpy as np
from jax import lax
from jax.experimental import pallas as pl
from jax.experimental.pallas import tpu as pltpu
from jax.sharding import PartitionSpec as P

MESH = pl.DeviceIdType.MESH
F32 = jnp.float32
BF16 = jnp.bfloat16
PAIR = 8
FACE = 4


def tables():
    order_index = np.arange(8)
    colloc = np.cos(np.pi * order_index / 7.0)
    end_weights = (
        np.where((order_index == 0) | (order_index == 7), 2.0, 1.0) * (-1.0) ** order_index
    )
    spacing = colloc[:, None] - colloc[None, :] + np.eye(8)
    raw_matrix = np.outer(end_weights, 1.0 / end_weights) / spacing
    off_part = raw_matrix * (1.0 - np.eye(8))
    derivative = 0.25 * (off_part - np.eye(8) * off_part.sum(axis=1)[:, None])
    derivative = derivative.astype(np.float32).astype(np.float64)
    eye2, eye8, eye16 = np.eye(2), np.eye(8), np.eye(16)

    def rows_matrix(mat):
        def part(out_low, in_low):
            return np.kron(mat[out_low::2, in_low::2], eye16)

        return np.block([[part(0, 0), part(0, 1)], [part(1, 1), part(1, 0)]])

    along_second = np.kron(eye2, np.kron(derivative, eye8)).T
    along_third = np.kron(eye16, derivative).T
    stack = [
        along_second,
        along_third,
        along_second.T,
        along_third.T,
        rows_matrix(derivative),
        rows_matrix(derivative.T),
    ]
    high = [np.asarray(m, np.float32).astype(jnp.bfloat16) for m in stack]
    low = [
        (np.asarray(m, np.float32) - h.astype(np.float32)).astype(jnp.bfloat16)
        for m, h in zip(stack, high)
    ]
    mats = np.stack(high + low)
    point_index = np.arange(512)
    corner_index = np.arange(8)
    sign_first = 1.0 - 2.0 * (corner_index >> 2 & 1)
    sign_second = 1.0 - 2.0 * (corner_index >> 1 & 1)
    sign_third = 1.0 - 2.0 * (corner_index & 1)
    node_first = colloc[point_index // 64][:, None]
    node_second = colloc[point_index // 8 % 8][:, None]
    node_third = colloc[point_index % 8][:, None]
    corner = (
        0.5
        * (1.0 + sign_first[None, :] * node_first)
        * (0.5 * (1.0 + sign_second[None, :] * node_second))
        * (0.5 * (1.0 + sign_third[None, :] * node_third))
    )
    return jnp.asarray(mats), jnp.asarray(corner.T, F32)


def kernel(
    ns,
    ng,
    right_ref,
    metric_ref,
    helm_ref,
    jac_ref,
    pair_ref,
    slots_ref,
    face_ref,
    map_ref,
    cinv_ref,
    mats_ref,
    corner_ref,
    sol_ref,
    res_ref,
    idx,
    hi_ref,
    lo_ref,
    ohlo,
    x_ref,
    val_ref,
    cscr,
    mcol,
    send_s,
    recv_s,
    send_f,
    recv_f,
    send_r,
    recv_r,
    send_b,
    recv_b,
    send_sem,
    recv_sem,
):
    g = lax.axis_index("grp")
    s = lax.axis_index("sub")
    nxt, prv = lax.rem(g + 1, ng), lax.rem(g + ng - 1, ng)
    rows = 2 * PAIR + ns + 2 * FACE
    tiles = rows // 8
    at_pair = ns + 2 * FACE

    recv_s[...] = jnp.zeros_like(recv_s)

    barrier = pltpu.get_barrier_semaphore()

    def greet_sub(k, carry):
        pl.semaphore_signal(
            barrier, inc=1, device_id={"sub": lax.rem(s + k, ns)}, device_id_type=MESH
        )
        return carry

    def greet_grp(k, carry):
        pl.semaphore_signal(
            barrier, inc=1, device_id={"grp": lax.rem(g + k, ng)}, device_id_type=MESH
        )
        return carry

    lax.fori_loop(1, ns, greet_sub, 0)
    lax.fori_loop(1, ng, greet_grp, 0)

    def cube(ref, base=0):
        return jnp.concatenate(
            [ref[:, base + 128 * k : base + 128 * (k + 1)] for k in range(4)], axis=0
        )

    def total(x):
        return jnp.sum(jnp.sum(x, axis=0, keepdims=True), axis=1, keepdims=True)

    lane = lax.broadcasted_iota(jnp.int32, (1, 128), 1)

    def pick(row, k):
        return jnp.sum(jnp.where(lane == k, row, 0.0), axis=1, keepdims=True)

    def put(k, value):
        return jnp.where(lane == k, value, 0.0)

    eye_16 = lax.broadcasted_iota(jnp.int32, (16, 16), 0) == lax.broadcasted_iota(
        jnp.int32, (16, 16), 1
    )
    lane_16 = lax.broadcasted_iota(jnp.int32, (16, 128), 1).astype(F32)
    for q in range(8):
        column = jnp.sum(
            jnp.where(eye_16, map_ref[q : q + 1, :].astype(F32), 0.0), axis=1, keepdims=True
        )
        mcol[q] = jnp.where(lane_16 == column, 1.0, 0.0)
    cscr[...] = jnp.zeros_like(cscr)
    cscr[:, :64] = cinv_ref[0]

    def restrict(x):
        row = jnp.zeros((1, 128), F32)
        for q in range(8):
            acc = x[:16] * corner_ref[q : q + 1, :128]
            for k in range(1, 4):
                acc += x[16 * k : 16 * (k + 1)] * corner_ref[q : q + 1, 128 * k : 128 * (k + 1)]
            vertex = jnp.sum(acc, axis=1, keepdims=True)
            row += jnp.sum(vertex * mcol[q], axis=0, keepdims=True)
        return row

    eye_64 = lax.broadcasted_iota(jnp.int32, (64, 128), 0) == lax.broadcasted_iota(
        jnp.int32, (64, 128), 1
    )

    def prolong(coarse):
        column = jnp.sum(jnp.where(eye_64, coarse, 0.0), axis=1, keepdims=True)
        solved = jnp.sum(cscr[...] * column, axis=0, keepdims=True)
        blocks = [jnp.zeros((16, 128), F32) for _ in range(4)]
        for q in range(8):
            at_vertex = jnp.sum(mcol[q] * solved, axis=1, keepdims=True)
            for k in range(4):
                blocks[k] += at_vertex * corner_ref[q : q + 1, 128 * k : 128 * (k + 1)]
        return jnp.concatenate(blocks, axis=0)

    def copy_sub(src, dst, sem, peer):
        return pltpu.make_async_remote_copy(
            src_ref=src,
            dst_ref=dst,
            send_sem=send_sem.at[sem],
            recv_sem=recv_sem.at[sem],
            device_id={"sub": peer},
            device_id_type=MESH,
        )

    def copy_grp(src, dst, sem, peer):
        return pltpu.make_async_remote_copy(
            src_ref=src,
            dst_ref=dst,
            send_sem=send_sem.at[sem],
            recv_sem=recv_sem.at[sem],
            device_id={"grp": peer},
            device_id_type=MESH,
        )

    def wait_bytes(ref, sem):
        pltpu.make_async_copy(ref, ref, sem).wait()

    def sum_sub_start(phase, row):
        send_r[phase] = row
        recv_r[phase, s] = row

        def go(k, carry):
            peer = lax.rem(s + k, ns)
            copy_sub(send_r.at[phase], recv_r.at[phase, s], 12 + phase, peer).start()
            return carry

        lax.fori_loop(1, ns, go, 0)

    def sum_sub(phase):
        wait_bytes(recv_r.at[phase, pl.ds(0, ns - 1)], recv_sem.at[12 + phase])
        return jnp.sum(recv_r[phase], axis=0)

    def sum_grp_start(phase, row):
        send_b[phase] = row
        recv_b[phase, g] = row

        def go(k, carry):
            peer = lax.rem(g + k, ng)
            copy_grp(send_b.at[phase], recv_b.at[phase, g], 16 + phase, peer).start()
            return carry

        lax.fori_loop(1, ng, go, 0)

    def sum_grp(phase):
        wait_bytes(recv_b.at[phase, pl.ds(0, ng - 1)], recv_sem.at[16 + phase])
        return jnp.sum(recv_b[phase], axis=0)

    residual = cube(right_ref)
    partial_coarse = restrict(residual)

    idx[:ns, :] = slots_ref[0]
    for k in range(2):
        for m in range(FACE):
            at = ns + FACE * k + m
            idx[at : at + 1, :] = face_ref[k : k + 1, 128 * m : 128 * (m + 1)]
        for m in range(PAIR):
            at = at_pair + PAIR * k + m
            idx[at : at + 1, :] = pair_ref[k : k + 1, 128 * m : 128 * (m + 1)]
    points = idx[...]
    row_of = ((points >> 7) & 3) * 16 + (points >> 9)
    hi_ref[...] = jnp.where(points >= 8192, 1024, row_of)
    lo_ref[...] = points & 127

    pl.semaphore_wait(barrier, ns + ng - 2)

    sum_sub_start(0, partial_coarse)

    sub_128 = lax.broadcasted_iota(jnp.int32, (128, 128), 0)
    sub_64 = lax.broadcasted_iota(jnp.int32, (64, 128), 0)

    def build(t, carry):
        low = lo_ref[pl.ds(pl.multiple_of(t * 8, 8), 8), :]
        ohlo[t] = jnp.concatenate(
            [jnp.where(sub_128 == low[r : r + 1], 1.0, 0.0).astype(BF16) for r in range(8)],
            axis=1,
        )
        return carry

    lax.fori_loop(0, tiles, build, 0)

    def gather(first, last):
        high = hi_ref[first:last, :]
        low = lo_ref[first:last, :]

        def step(t, acc):
            block = x_ref[pl.ds(pl.multiple_of(t * 8, 8), 8), :]
            for r in range(8):
                row = jnp.broadcast_to(block[r : r + 1], (last - first, 128))
                got = jnp.take_along_axis(row, low, axis=1, mode="promise_in_bounds")
                acc = jnp.where(high == t * 8 + r, got, acc)
            return acc

        return lax.fori_loop(0, 8, step, jnp.zeros((last - first, 128), F32))

    def scatter(first, last, acc):
        def step(t, acc):
            at = pl.ds(pl.multiple_of(t * 8, 8), 8)
            high = hi_ref[at, :]
            value = val_ref[at, :]
            upper = value.astype(BF16).astype(F32)
            lower = value - upper
            parts = []
            for r in range(8):
                hit = sub_64 == high[r : r + 1]
                parts.append(
                    jnp.concatenate(
                        [
                            jnp.where(hit, upper[r : r + 1], 0.0),
                            jnp.where(hit, lower[r : r + 1], 0.0),
                        ],
                        axis=0,
                    ).astype(BF16)
                )
            left = jnp.concatenate(parts, axis=1)
            return acc + lax.dot_general(
                left, ohlo[t], (((1,), (1,)), ((), ())), preferred_element_type=F32
            )

        return lax.fori_loop(first, last, step, acc)

    def assemble(phase, x, meanwhile=lambda: None, before_slots=lambda: None):
        x_ref[...] = x
        got = gather(0, at_pair)
        send_s[phase] = got[:ns].reshape(ns, 1, 128)
        send_f[phase, 0] = got[ns : ns + FACE]
        send_f[phase, 1] = got[ns + FACE :]

        def go(k, carry):
            peer = lax.rem(s + k, ns)
            copy_sub(send_s.at[phase, peer], recv_s.at[phase, s], phase, peer).start()
            return carry

        lax.fori_loop(1, ns, go, 0)
        down = copy_grp(send_f.at[phase, 0], recv_f.at[phase, 1], 4 + phase, prv)
        up = copy_grp(send_f.at[phase, 1], recv_f.at[phase, 0], 8 + phase, nxt)
        down.start()
        up.start()
        meanwhile()
        got = gather(at_pair, rows)
        val_ref[at_pair : at_pair + PAIR, :] = got[PAIR:]
        val_ref[at_pair + PAIR :, :] = got[:PAIR]
        acc = scatter(at_pair // 8, tiles, jnp.zeros((128, 128), F32))
        down.wait_recv()
        up.wait_recv()
        val_ref[ns : ns + FACE, :] = jnp.where(g == 0, 0.0, recv_f[phase, 0])
        val_ref[ns + FACE : at_pair, :] = jnp.where(g == ng - 1, 0.0, recv_f[phase, 1])
        acc = scatter(ns // 8, at_pair // 8, acc)
        before_slots()
        wait_bytes(recv_s.at[phase, pl.ds(0, ns - 1)], recv_sem.at[phase])
        val_ref[:ns, :] = recv_s[phase].reshape(ns, 128)
        acc = scatter(0, ns // 8, acc)
        return x + acc[:64] + acc[64:]

    def split(x):
        upper = x.astype(BF16)
        return upper, (x - upper.astype(F32)).astype(BF16)

    def dot(a, b):
        return jnp.dot(a, b, preferred_element_type=F32)

    def dot_right(x, k):
        upper, lower = split(x)
        both = dot(jnp.concatenate([upper, lower], axis=0), mats_ref[k])
        return both[:64] + both[64:] + dot(upper, mats_ref[k + 6])

    left_half = lax.broadcasted_iota(jnp.int32, (64, 128), 1) < 64

    def dot_rows(x, k):
        upper, lower = split(jnp.concatenate([x, pltpu.roll(x, 64, 1)], axis=0))
        both = dot(mats_ref[k], jnp.concatenate([upper, lower], axis=1))
        out = both[:, :128] + both[:, 128:] + dot(mats_ref[k + 6], upper)
        return jnp.where(left_half, out[:64], out[64:])

    def stiffness(x):
        flux_first = cube(metric_ref, 0) * dot_rows(x, 4)
        flux_second = cube(metric_ref, 512) * dot_right(x, 0)
        flux_third = cube(metric_ref, 1024) * dot_right(x, 1)
        return dot_rows(flux_first, 5) + dot_right(flux_second, 2) + dot_right(flux_third, 3)

    right = residual
    first = cube(jac_ref) * right + prolong(sum_sub(0))
    summed = assemble(0, first)
    inner = stiffness(summed)
    mass = cube(helm_ref) * first

    def first_sums():
        row = put(0, total(right * first)) + put(1, total(summed * inner + first * mass))
        sum_sub_start(1, row)

    image = assemble(1, inner, first_sums)
    image += mass
    sum_sub_start(2, restrict(image))
    sum_grp_start(0, sum_sub(1))
    second = cube(jac_ref) * image + prolong(sum_sub(2))
    summed_second = assemble(2, second)
    inner_second = stiffness(summed_second)
    sums = sum_grp(0)
    rz_first, curved = pick(sums, 0), pick(sums, 1)
    alpha = rz_first / curved
    residual = right - alpha * image
    smoothed = first - alpha * second
    row = (
        put(0, total(residual * smoothed))
        + put(1, total(smoothed * image))
        + put(
            2,
            total(
                (summed - alpha * summed_second) * (inner - alpha * inner_second)
                + smoothed * (cube(helm_ref) * smoothed)
            ),
        )
    )
    sum_sub_start(3, row)

    def last_sums():
        sum_grp_start(1, sum_sub(3))

    image_second = assemble(3, inner_second, before_slots=last_sums)
    image_second += cube(helm_ref) * second
    sums = sum_grp(1)
    rz_second = pick(sums, 0)
    beta = rz_second / rz_first
    curve = pick(sums, 2) + 2.0 * beta * pick(sums, 1) + beta * beta * curved
    alpha_last = rz_second / curve
    solved = alpha * first + alpha_last * (smoothed + beta * first)
    residual = residual - alpha_last * (image - alpha * image_second + beta * image)
    for k in range(4):
        sol_ref[:, 128 * k : 128 * (k + 1)] = solved[16 * k : 16 * (k + 1)]
        res_ref[:, 128 * k : 128 * (k + 1)] = residual[16 * k : 16 * (k + 1)]

    for phase in range(4):
        wait_bytes(send_s.at[phase, pl.ds(0, ns - 1)], send_sem.at[phase])
        wait_bytes(send_f.at[phase, 0], send_sem.at[4 + phase])
        wait_bytes(send_f.at[phase, 1], send_sem.at[8 + phase])
    for phase in range(4):
        wait_bytes(recv_r.at[phase, pl.ds(0, ns - 1)], send_sem.at[12 + phase])
    for phase in range(2):
        wait_bytes(recv_b.at[phase, pl.ds(0, ng - 1)], send_sem.at[16 + phase])


def body(ns, ng, *args):
    mats, corner = tables()
    rows = 2 * PAIR + ns + 2 * FACE
    vmem = pl.BlockSpec(memory_space=pltpu.VMEM)
    shape = jax.ShapeDtypeStruct((16, 512), F32)
    return pl.pallas_call(
        functools.partial(kernel, ns, ng),
        out_shape=(shape, shape),
        in_specs=[vmem] * 11,
        out_specs=(vmem, vmem),
        scratch_shapes=[
            pltpu.VMEM((rows, 128), jnp.int32),
            pltpu.VMEM((rows, 128), jnp.int32),
            pltpu.VMEM((rows, 128), jnp.int32),
            pltpu.VMEM((rows // 8, 128, 1024), BF16),
            pltpu.VMEM((64, 128), F32),
            pltpu.VMEM((rows, 128), F32),
            pltpu.VMEM((64, 128), F32),
            pltpu.VMEM((8, 16, 128), F32),
            pltpu.VMEM((4, ns, 1, 128), F32),
            pltpu.VMEM((4, ns, 1, 128), F32),
            pltpu.VMEM((4, 2, FACE, 128), F32),
            pltpu.VMEM((4, 2, FACE, 128), F32),
            pltpu.VMEM((4, 1, 128), F32),
            pltpu.VMEM((4, ns, 1, 128), F32),
            pltpu.VMEM((2, 1, 128), F32),
            pltpu.VMEM((2, ng, 1, 128), F32),
            pltpu.SemaphoreType.DMA((18,)),
            pltpu.SemaphoreType.DMA((18,)),
        ],
        compiler_params=pltpu.CompilerParams(collective_id=0, has_side_effects=True),
    )(*args, mats, corner)


def solution(mesh):
    in_specs = (
        P(("grp", "sub"), None),
        P(("grp", "sub"), None),
        P(("grp", "sub"), None),
        P(("grp", "sub"), None),
        P(None, ("grp", "sub")),
        P(("grp", "sub"), None, None),
        P(None, ("grp", "sub")),
        P(None, ("grp", "sub")),
        P("grp", None, None),
    )
    out_specs = (P(("grp", "sub"), None), P(("grp", "sub"), None))
    return jax.shard_map(
        functools.partial(body, mesh.shape["sub"], mesh.shape["grp"]),
        mesh=mesh,
        in_specs=in_specs,
        out_specs=out_specs,
        check_vma=False,
    )
```

```python
import functools

import jax
import jax.numpy as jnp
import numpy as np
from jax import lax
from jax.experimental import pallas as pl
from jax.experimental.pallas import tpu as pltpu
from jax.sharding import PartitionSpec as P

MESH = pl.DeviceIdType.MESH
F32 = jnp.float32
BF16 = jnp.bfloat16
PAIR = 8
FACE = 4


def tables():
    order_index = np.arange(8)
    colloc = np.cos(np.pi * order_index / 7.0)
    end_weights = (
        np.where((order_index == 0) | (order_index == 7), 2.0, 1.0) * (-1.0) ** order_index
    )
    spacing = colloc[:, None] - colloc[None, :] + np.eye(8)
    raw_matrix = np.outer(end_weights, 1.0 / end_weights) / spacing
    off_part = raw_matrix * (1.0 - np.eye(8))
    derivative = 0.25 * (off_part - np.eye(8) * off_part.sum(axis=1)[:, None])
    derivative = derivative.astype(np.float32).astype(np.float64)
    eye2, eye8, eye16 = np.eye(2), np.eye(8), np.eye(16)

    def rows_matrix(mat):
        def part(out_low, in_low):
            return np.kron(mat[out_low::2, in_low::2], eye16)

        return np.block([[part(0, 0), part(0, 1)], [part(1, 1), part(1, 0)]])

    along_second = np.kron(eye2, np.kron(derivative, eye8)).T
    along_third = np.kron(eye16, derivative).T
    stack = [
        along_second,
        along_third,
        along_second.T,
        along_third.T,
        rows_matrix(derivative),
        rows_matrix(derivative.T),
    ]
    high = [np.asarray(m, np.float32).astype(jnp.bfloat16) for m in stack]
    low = [
        (np.asarray(m, np.float32) - h.astype(np.float32)).astype(jnp.bfloat16)
        for m, h in zip(stack, high)
    ]
    mats = np.stack(high + low)
    point_index = np.arange(512)
    corner_index = np.arange(8)
    sign_first = 1.0 - 2.0 * (corner_index >> 2 & 1)
    sign_second = 1.0 - 2.0 * (corner_index >> 1 & 1)
    sign_third = 1.0 - 2.0 * (corner_index & 1)
    node_first = colloc[point_index // 64][:, None]
    node_second = colloc[point_index // 8 % 8][:, None]
    node_third = colloc[point_index % 8][:, None]
    corner = (
        0.5
        * (1.0 + sign_first[None, :] * node_first)
        * (0.5 * (1.0 + sign_second[None, :] * node_second))
        * (0.5 * (1.0 + sign_third[None, :] * node_third))
    )
    factors = np.zeros((8, 512))
    factors[0, :8] = 0.5 * (1.0 + colloc)
    factors[0, 8:16] = 0.5 * (1.0 - colloc)
    return jnp.asarray(mats), jnp.asarray(np.concatenate([corner.T, factors]), F32)


def kernel(
    ns,
    ng,
    right_ref,
    metric_ref,
    helm_ref,
    jac_ref,
    pair_ref,
    slots_ref,
    face_ref,
    map_ref,
    cinv_ref,
    mats_ref,
    corner_ref,
    sol_ref,
    res_ref,
    idx,
    hi_ref,
    lo_ref,
    ohlo,
    x_ref,
    val_ref,
    cscr,
    mcol,
    send_s,
    recv_s,
    send_f,
    recv_f,
    send_r,
    recv_r,
    send_b,
    recv_b,
    send_h,
    recv_h,
    send_t,
    recv_t,
    map_scr,
    phi,
    send_sem,
    recv_sem,
):
    g = lax.axis_index("grp")
    s = lax.axis_index("sub")
    nxt, prv = lax.rem(g + 1, ng), lax.rem(g + ng - 1, ng)
    rows = 2 * PAIR + ns + 2 * FACE
    tiles = rows // 8
    at_pair = ns + 2 * FACE

    recv_s[...] = jnp.zeros_like(recv_s)
    recv_h[...] = jnp.zeros_like(recv_h)
    recv_t[...] = jnp.zeros_like(recv_t)

    barrier = pltpu.get_barrier_semaphore()

    def greet_sub(k, carry):
        pl.semaphore_signal(
            barrier, inc=1, device_id={"sub": lax.rem(s + k, ns)}, device_id_type=MESH
        )
        return carry

    def greet_grp(k, carry):
        pl.semaphore_signal(
            barrier, inc=1, device_id={"grp": lax.rem(g + k, ng)}, device_id_type=MESH
        )
        return carry

    lax.fori_loop(1, ns, greet_sub, 0)
    lax.fori_loop(1, ng, greet_grp, 0)

    def cube(ref, base=0):
        return jnp.concatenate(
            [ref[:, base + 128 * k : base + 128 * (k + 1)] for k in range(4)], axis=0
        )

    def total(x):
        return jnp.sum(jnp.sum(x, axis=0, keepdims=True), axis=1, keepdims=True)

    lane = lax.broadcasted_iota(jnp.int32, (1, 128), 1)

    def pick(row, k):
        return jnp.sum(jnp.where(lane == k, row, 0.0), axis=1, keepdims=True)

    def put(k, value):
        return jnp.where(lane == k, value, 0.0)

    eye_16 = lax.broadcasted_iota(jnp.int32, (16, 16), 0) == lax.broadcasted_iota(
        jnp.int32, (16, 16), 1
    )
    lane_16 = lax.broadcasted_iota(jnp.int32, (16, 128), 1).astype(F32)
    for q in range(8):
        column = jnp.sum(
            jnp.where(eye_16, map_ref[q : q + 1, :].astype(F32), 0.0), axis=1, keepdims=True
        )
        mcol[q] = jnp.where(lane_16 == column, 1.0, 0.0)
    cscr[...] = jnp.zeros_like(cscr)
    cscr[:, :64] = cinv_ref[0]

    def restrict(x):
        row = jnp.zeros((1, 128), F32)
        for q in range(8):
            acc = x[:16] * corner_ref[q : q + 1, :128]
            for k in range(1, 4):
                acc += x[16 * k : 16 * (k + 1)] * corner_ref[q : q + 1, 128 * k : 128 * (k + 1)]
            vertex = jnp.sum(acc, axis=1, keepdims=True)
            row += jnp.sum(vertex * mcol[q], axis=0, keepdims=True)
        return row

    eye_64 = lax.broadcasted_iota(jnp.int32, (64, 128), 0) == lax.broadcasted_iota(
        jnp.int32, (64, 128), 1
    )

    def solve(coarse):
        column = jnp.sum(jnp.where(eye_64, coarse, 0.0), axis=1, keepdims=True)
        return jnp.sum(cscr[...] * column, axis=0, keepdims=True)

    def prolong(solved):
        blocks = [jnp.zeros((16, 128), F32) for _ in range(4)]
        for q in range(8):
            at_vertex = jnp.sum(mcol[q] * solved, axis=1, keepdims=True)
            for k in range(4):
                blocks[k] += at_vertex * corner_ref[q : q + 1, 128 * k : 128 * (k + 1)]
        return jnp.concatenate(blocks, axis=0)

    def copy_sub(src, dst, sem, peer):
        return pltpu.make_async_remote_copy(
            src_ref=src,
            dst_ref=dst,
            send_sem=send_sem.at[sem],
            recv_sem=recv_sem.at[sem],
            device_id={"sub": peer},
            device_id_type=MESH,
        )

    def copy_grp(src, dst, sem, peer):
        return pltpu.make_async_remote_copy(
            src_ref=src,
            dst_ref=dst,
            send_sem=send_sem.at[sem],
            recv_sem=recv_sem.at[sem],
            device_id={"grp": peer},
            device_id_type=MESH,
        )

    def wait_bytes(ref, sem):
        pltpu.make_async_copy(ref, ref, sem).wait()

    def sum_sub_start(phase, row):
        send_r[phase] = row
        recv_r[phase, s] = row

        def go(k, carry):
            peer = lax.rem(s + k, ns)
            copy_sub(send_r.at[phase], recv_r.at[phase, s], 12 + phase, peer).start()
            return carry

        lax.fori_loop(1, ns, go, 0)

    def sum_sub(phase):
        wait_bytes(recv_r.at[phase, pl.ds(0, ns - 1)], recv_sem.at[12 + phase])
        return jnp.sum(recv_r[phase], axis=0)

    def sum_grp_start(phase, row):
        send_b[phase] = row
        recv_b[phase, g] = row

        def go(k, carry):
            peer = lax.rem(g + k, ng)
            copy_grp(send_b.at[phase], recv_b.at[phase, g], 16 + phase, peer).start()
            return carry

        lax.fori_loop(1, ng, go, 0)

    def sum_grp(phase):
        wait_bytes(recv_b.at[phase, pl.ds(0, ng - 1)], recv_sem.at[16 + phase])
        return jnp.sum(recv_b[phase], axis=0)

    residual = cube(right_ref)
    partial_coarse = restrict(residual)

    idx[:ns, :] = slots_ref[0]
    for k in range(2):
        for m in range(FACE):
            at = ns + FACE * k + m
            idx[at : at + 1, :] = face_ref[k : k + 1, 128 * m : 128 * (m + 1)]
        for m in range(PAIR):
            at = at_pair + PAIR * k + m
            idx[at : at + 1, :] = pair_ref[k : k + 1, 128 * m : 128 * (m + 1)]
    points = idx[...]
    row_of = ((points >> 7) & 3) * 16 + (points >> 9)
    hi_ref[...] = jnp.where(points >= 8192, 1024, row_of)
    lo_ref[...] = points & 127

    def gather(first, last):
        high = hi_ref[first:last, :]
        low = lo_ref[first:last, :]

        def step(t, acc):
            block = x_ref[pl.ds(pl.multiple_of(t * 8, 8), 8), :]
            for r in range(8):
                row = jnp.broadcast_to(block[r : r + 1], (last - first, 128))
                got = jnp.take_along_axis(row, low, axis=1, mode="promise_in_bounds")
                acc = jnp.where(high == t * 8 + r, got, acc)
            return acc

        return lax.fori_loop(0, 8, step, jnp.zeros((last - first, 128), F32))

    def look(table, at):
        return jnp.take_along_axis(table, at, axis=1, mode="promise_in_bounds")

    map_scr[...] = jnp.zeros_like(map_scr)
    map_scr[:, :16] = map_ref[...]
    lane_8 = lax.broadcasted_iota(jnp.int32, (8, 128), 1)
    corner_row = lax.broadcasted_iota(jnp.int32, (8, 128), 0) == lane_8 >> 4
    spread = look(map_scr[...], lane_8 & 15).astype(F32)
    map_row = jnp.sum(jnp.where(corner_row, spread, 0.0), axis=0, keepdims=True)
    x_ref[...] = cube(jac_ref) * residual
    send_h[:, :, :128] = jnp.broadcast_to(partial_coarse.reshape(1, 1, 128), (ns, 1, 128))
    send_h[:, :, 128:] = gather(0, ns).reshape(ns, 1, 128)
    send_t[:, :, :128] = jnp.broadcast_to(
        map_row.astype(jnp.int32).reshape(1, 1, 128), (ns, 1, 128)
    )
    send_t[:, :, 128:] = points[:ns].reshape(ns, 1, 128)
    recv_h[s, :, :128] = partial_coarse

    pl.semaphore_wait(barrier, ns + ng - 2)

    def hello(k, carry):
        peer = lax.rem(s + k, ns)
        copy_sub(send_h.at[peer], recv_h.at[s], 18, peer).start()
        copy_sub(send_t.at[peer], recv_t.at[s], 19, peer).start()
        return carry

    lax.fori_loop(1, ns, hello, 0)

    sub_128 = lax.broadcasted_iota(jnp.int32, (128, 128), 0)
    sub_64 = lax.broadcasted_iota(jnp.int32, (64, 128), 0)

    def build(t, carry):
        low = lo_ref[pl.ds(pl.multiple_of(t * 8, 8), 8), :]
        ohlo[t] = jnp.concatenate(
            [jnp.where(sub_128 == low[r : r + 1], 1.0, 0.0).astype(BF16) for r in range(8)],
            axis=1,
        )
        return carry

    lax.fori_loop(0, tiles, build, 0)

    def scatter(first, last, acc):
        def step(t, acc):
            at = pl.ds(pl.multiple_of(t * 8, 8), 8)
            high = hi_ref[at, :]
            value = val_ref[at, :]
            upper = value.astype(BF16).astype(F32)
            lower = value - upper
            parts = []
            for r in range(8):
                hit = sub_64 == high[r : r + 1]
                parts.append(
                    jnp.concatenate(
                        [
                            jnp.where(hit, upper[r : r + 1], 0.0),
                            jnp.where(hit, lower[r : r + 1], 0.0),
                        ],
                        axis=0,
                    ).astype(BF16)
                )
            left = jnp.concatenate(parts, axis=1)
            return acc + lax.dot_general(
                left, ohlo[t], (((1,), (1,)), ((), ())), preferred_element_type=F32
            )

        return lax.fori_loop(first, last, step, acc)

    def send_slots(phase):
        send_s[phase] = gather(0, ns).reshape(ns, 1, 128)

        def go(k, carry):
            peer = lax.rem(s + k, ns)
            copy_sub(send_s.at[phase, peer], recv_s.at[phase, s], phase, peer).start()
            return carry

        lax.fori_loop(1, ns, go, 0)

    def send_faces(phase):
        got = gather(ns, at_pair)
        send_f[phase, 0] = got[:FACE]
        send_f[phase, 1] = got[FACE:]
        down = copy_grp(send_f.at[phase, 0], recv_f.at[phase, 1], 4 + phase, prv)
        up = copy_grp(send_f.at[phase, 1], recv_f.at[phase, 0], 8 + phase, nxt)
        down.start()
        up.start()
        return down, up

    def add_pairs():
        got = gather(at_pair, rows)
        val_ref[at_pair : at_pair + PAIR, :] = got[PAIR:]
        val_ref[at_pair + PAIR :, :] = got[:PAIR]
        return scatter(at_pair // 8, tiles, jnp.zeros((128, 128), F32))

    def add_faces(phase, copies, acc):
        for copy in copies:
            copy.wait_recv()
        val_ref[ns : ns + FACE, :] = jnp.where(g == 0, 0.0, recv_f[phase, 0])
        val_ref[ns + FACE : at_pair, :] = jnp.where(g == ng - 1, 0.0, recv_f[phase, 1])
        return scatter(ns // 8, at_pair // 8, acc)

    def wait_slots(phase):
        wait_bytes(recv_s.at[phase, pl.ds(0, ns - 1)], recv_sem.at[phase])
        return recv_s[phase].reshape(ns, 128)

    def add_slots(value, acc):
        val_ref[:ns, :] = value
        return scatter(0, ns // 8, acc)

    def assemble(phase, x, meanwhile=lambda: None, before_slots=lambda: None):
        x_ref[...] = x
        send_slots(phase)
        copies = send_faces(phase)
        meanwhile()
        acc = add_faces(phase, copies, add_pairs())
        before_slots()
        acc = add_slots(wait_slots(phase), acc)
        return x + acc[:64] + acc[64:]

    def assemble_known(phase, x, slot_values):
        x_ref[...] = x
        copies = send_faces(phase)
        acc = add_slots(slot_values, add_pairs())
        acc = add_faces(phase, copies, acc)
        return x + acc[:64] + acc[64:]

    def peer_points():
        return recv_t[:, :, 128:].reshape(ns, 128)

    def corner_functions():
        point = peer_points()
        table = jnp.broadcast_to(corner_ref[8:9, :128], (ns, 128))
        nodes = [(point >> 6) & 7, (point >> 3) & 7, point & 7]
        near = [[look(table, node + 8 * bit) for bit in range(2)] for node in nodes]
        for q in range(8):
            phi[q] = near[0][q >> 2 & 1] * near[1][q >> 1 & 1] * near[2][q & 1]

    def coarse_at_peers(solved):
        corners = look(jnp.broadcast_to(solved, (ns, 128)), recv_t[:, :, :128].reshape(ns, 128))
        element = (peer_points() >> 9) & 15
        out = jnp.zeros((ns, 128), F32)
        for q in range(8):
            out += phi[q] * look(corners, element + 16 * q)
        return out

    def split(x):
        upper = x.astype(BF16)
        return upper, (x - upper.astype(F32)).astype(BF16)

    def dot(a, b):
        return jnp.dot(a, b, preferred_element_type=F32)

    def dot_right(x, k):
        upper, lower = split(x)
        both = dot(jnp.concatenate([upper, lower], axis=0), mats_ref[k])
        return both[:64] + both[64:] + dot(upper, mats_ref[k + 6])

    left_half = lax.broadcasted_iota(jnp.int32, (64, 128), 1) < 64

    def dot_rows(x, k):
        upper, lower = split(jnp.concatenate([x, pltpu.roll(x, 64, 1)], axis=0))
        both = dot(mats_ref[k], jnp.concatenate([upper, lower], axis=1))
        out = both[:, :128] + both[:, 128:] + dot(mats_ref[k + 6], upper)
        return jnp.where(left_half, out[:64], out[64:])

    def stiffness(x):
        flux_first = cube(metric_ref, 0) * dot_rows(x, 4)
        flux_second = cube(metric_ref, 512) * dot_right(x, 0)
        flux_third = cube(metric_ref, 1024) * dot_right(x, 1)
        return dot_rows(flux_first, 5) + dot_right(flux_second, 2) + dot_right(flux_third, 3)

    right = residual
    part = cube(jac_ref) * right
    wait_bytes(recv_t.at[pl.ds(0, ns - 1)], recv_sem.at[19])
    corner_functions()
    wait_bytes(recv_h.at[pl.ds(0, ns - 1)], recv_sem.at[18])
    solved = solve(jnp.sum(recv_h[:, :, :128], axis=0))
    first = part + prolong(solved)
    summed = assemble_known(
        0, first, recv_h[:, :, 128:].reshape(ns, 128) + coarse_at_peers(solved)
    )
    inner = stiffness(summed)
    mass = cube(helm_ref) * first

    def first_sums():
        row = put(0, total(right * first)) + put(1, total(summed * inner + first * mass))
        sum_sub_start(1, row)

    image = assemble(1, inner, first_sums)
    image += mass
    sum_sub_start(2, restrict(image))
    part = cube(jac_ref) * image
    x_ref[...] = part
    send_slots(2)
    sum_grp_start(0, sum_sub(1))
    solved = solve(sum_sub(2))
    second = part + prolong(solved)
    known = coarse_at_peers(solved)
    summed_second = assemble_known(2, second, wait_slots(2) + known)
    inner_second = stiffness(summed_second)
    sums = sum_grp(0)
    rz_first, curved = pick(sums, 0), pick(sums, 1)
    alpha = rz_first / curved
    residual = right - alpha * image
    smoothed = first - alpha * second
    row = (
        put(0, total(residual * smoothed))
        + put(1, total(smoothed * image))
        + put(
            2,
            total(
                (summed - alpha * summed_second) * (inner - alpha * inner_second)
                + smoothed * (cube(helm_ref) * smoothed)
            ),
        )
    )
    sum_sub_start(3, row)

    def last_sums():
        sum_grp_start(1, sum_sub(3))

    image_second = assemble(3, inner_second, before_slots=last_sums)
    image_second += cube(helm_ref) * second
    sums = sum_grp(1)
    rz_second = pick(sums, 0)
    beta = rz_second / rz_first
    curve = pick(sums, 2) + 2.0 * beta * pick(sums, 1) + beta * beta * curved
    alpha_last = rz_second / curve
    solved = alpha * first + alpha_last * (smoothed + beta * first)
    residual = residual - alpha_last * (image - alpha * image_second + beta * image)
    for k in range(4):
        sol_ref[:, 128 * k : 128 * (k + 1)] = solved[16 * k : 16 * (k + 1)]
        res_ref[:, 128 * k : 128 * (k + 1)] = residual[16 * k : 16 * (k + 1)]

    for phase in range(1, 4):
        wait_bytes(send_s.at[phase, pl.ds(0, ns - 1)], send_sem.at[phase])
    for phase in range(4):
        wait_bytes(send_f.at[phase, 0], send_sem.at[4 + phase])
        wait_bytes(send_f.at[phase, 1], send_sem.at[8 + phase])
    wait_bytes(send_h.at[pl.ds(0, ns - 1)], send_sem.at[18])
    wait_bytes(send_t.at[pl.ds(0, ns - 1)], send_sem.at[19])
    for phase in range(1, 4):
        wait_bytes(recv_r.at[phase, pl.ds(0, ns - 1)], send_sem.at[12 + phase])
    for phase in range(2):
        wait_bytes(recv_b.at[phase, pl.ds(0, ng - 1)], send_sem.at[16 + phase])


def body(ns, ng, *args):
    mats, corner = tables()
    rows = 2 * PAIR + ns + 2 * FACE
    vmem = pl.BlockSpec(memory_space=pltpu.VMEM)
    shape = jax.ShapeDtypeStruct((16, 512), F32)
    return pl.pallas_call(
        functools.partial(kernel, ns, ng),
        out_shape=(shape, shape),
        in_specs=[vmem] * 11,
        out_specs=(vmem, vmem),
        scratch_shapes=[
            pltpu.VMEM((rows, 128), jnp.int32),
            pltpu.VMEM((rows, 128), jnp.int32),
            pltpu.VMEM((rows, 128), jnp.int32),
            pltpu.VMEM((rows // 8, 128, 1024), BF16),
            pltpu.VMEM((64, 128), F32),
            pltpu.VMEM((rows, 128), F32),
            pltpu.VMEM((64, 128), F32),
            pltpu.VMEM((8, 16, 128), F32),
            pltpu.VMEM((4, ns, 1, 128), F32),
            pltpu.VMEM((4, ns, 1, 128), F32),
            pltpu.VMEM((4, 2, FACE, 128), F32),
            pltpu.VMEM((4, 2, FACE, 128), F32),
            pltpu.VMEM((4, 1, 128), F32),
            pltpu.VMEM((4, ns, 1, 128), F32),
            pltpu.VMEM((2, 1, 128), F32),
            pltpu.VMEM((2, ng, 1, 128), F32),
            pltpu.VMEM((ns, 1, 256), F32),
            pltpu.VMEM((ns, 1, 256), F32),
            pltpu.VMEM((ns, 1, 256), jnp.int32),
            pltpu.VMEM((ns, 1, 256), jnp.int32),
            pltpu.VMEM((8, 128), jnp.int32),
            pltpu.VMEM((8, ns, 128), F32),
            pltpu.SemaphoreType.DMA((20,)),
            pltpu.SemaphoreType.DMA((20,)),
        ],
        compiler_params=pltpu.CompilerParams(collective_id=0, has_side_effects=True),
    )(*args, mats, corner)


def solution(mesh):
    in_specs = (
        P(("grp", "sub"), None),
        P(("grp", "sub"), None),
        P(("grp", "sub"), None),
        P(("grp", "sub"), None),
        P(None, ("grp", "sub")),
        P(("grp", "sub"), None, None),
        P(None, ("grp", "sub")),
        P(None, ("grp", "sub")),
        P("grp", None, None),
    )
    out_specs = (P(("grp", "sub"), None), P(("grp", "sub"), None))
    return jax.shard_map(
        functools.partial(body, mesh.shape["sub"], mesh.shape["grp"]),
        mesh=mesh,
        in_specs=in_specs,
        out_specs=out_specs,
        check_vma=False,
    )
```

```python
import functools

import jax
import jax.numpy as jnp
import numpy as np
from jax import lax
from jax.experimental import pallas as pl
from jax.experimental.pallas import tpu as pltpu
from jax.sharding import PartitionSpec as P

MESH = pl.DeviceIdType.MESH
F32 = jnp.float32
BF16 = jnp.bfloat16
PAIR = 8
FACE = 4


def tables():
    order_index = np.arange(8)
    colloc = np.cos(np.pi * order_index / 7.0)
    end_weights = (
        np.where((order_index == 0) | (order_index == 7), 2.0, 1.0) * (-1.0) ** order_index
    )
    spacing = colloc[:, None] - colloc[None, :] + np.eye(8)
    raw_matrix = np.outer(end_weights, 1.0 / end_weights) / spacing
    off_part = raw_matrix * (1.0 - np.eye(8))
    derivative = 0.25 * (off_part - np.eye(8) * off_part.sum(axis=1)[:, None])
    derivative = derivative.astype(np.float32).astype(np.float64)
    eye2, eye8, eye16 = np.eye(2), np.eye(8), np.eye(16)

    def rows_matrix(mat):
        def part(out_low, in_low):
            return np.kron(mat[out_low::2, in_low::2], eye16)

        return np.block([[part(0, 0), part(0, 1)], [part(1, 1), part(1, 0)]])

    along_second = np.kron(eye2, np.kron(derivative, eye8)).T
    along_third = np.kron(eye16, derivative).T
    stack = [
        along_second,
        along_third,
        along_second.T,
        along_third.T,
        rows_matrix(derivative),
        rows_matrix(derivative.T),
    ]
    high = [np.asarray(m, np.float32).astype(jnp.bfloat16) for m in stack]
    low = [
        (np.asarray(m, np.float32) - h.astype(np.float32)).astype(jnp.bfloat16)
        for m, h in zip(stack, high)
    ]
    mats = np.stack(high + low)
    point_index = np.arange(512)
    corner_index = np.arange(8)
    sign_first = 1.0 - 2.0 * (corner_index >> 2 & 1)
    sign_second = 1.0 - 2.0 * (corner_index >> 1 & 1)
    sign_third = 1.0 - 2.0 * (corner_index & 1)
    node_first = colloc[point_index // 64][:, None]
    node_second = colloc[point_index // 8 % 8][:, None]
    node_third = colloc[point_index % 8][:, None]
    corner = (
        0.5
        * (1.0 + sign_first[None, :] * node_first)
        * (0.5 * (1.0 + sign_second[None, :] * node_second))
        * (0.5 * (1.0 + sign_third[None, :] * node_third))
    )
    factors = np.zeros((8, 512))
    factors[0, :8] = 0.5 * (1.0 + colloc)
    factors[0, 8:16] = 0.5 * (1.0 - colloc)
    return jnp.asarray(mats), jnp.asarray(np.concatenate([corner.T, factors]), F32)


def kernel(
    ns,
    ng,
    right_ref,
    metric_ref,
    helm_ref,
    jac_ref,
    pair_ref,
    slots_ref,
    face_ref,
    map_ref,
    cinv_ref,
    mats_ref,
    corner_ref,
    sol_ref,
    res_ref,
    idx,
    hi_ref,
    lo_ref,
    ohlo,
    x_ref,
    val_ref,
    cscr,
    mcol,
    send_s,
    recv_s,
    send_f,
    recv_f,
    send_r,
    recv_r,
    send_b,
    recv_b,
    send_h,
    recv_h,
    send_t,
    recv_t,
    map_scr,
    phi,
    send_sem,
    recv_sem,
):
    g = lax.axis_index("grp")
    s = lax.axis_index("sub")
    nxt, prv = lax.rem(g + 1, ng), lax.rem(g + ng - 1, ng)
    rows = 2 * PAIR + ns + 2 * FACE
    tiles = rows // 8
    at_pair = ns + 2 * FACE

    recv_s[...] = jnp.zeros_like(recv_s)
    recv_h[...] = jnp.zeros_like(recv_h)
    recv_t[...] = jnp.zeros_like(recv_t)

    barrier = pltpu.get_barrier_semaphore()

    def greet_sub(k, carry):
        pl.semaphore_signal(
            barrier, inc=1, device_id={"sub": lax.rem(s + k, ns)}, device_id_type=MESH
        )
        return carry

    def greet_grp(k, carry):
        pl.semaphore_signal(
            barrier, inc=1, device_id={"grp": lax.rem(g + k, ng)}, device_id_type=MESH
        )
        return carry

    lax.fori_loop(1, ns, greet_sub, 0, unroll=True)
    lax.fori_loop(1, ng, greet_grp, 0, unroll=True)

    def cube(ref, base=0):
        return jnp.concatenate(
            [ref[:, base + 128 * k : base + 128 * (k + 1)] for k in range(4)], axis=0
        )

    def total(x):
        return jnp.sum(jnp.sum(x, axis=0, keepdims=True), axis=1, keepdims=True)

    lane = lax.broadcasted_iota(jnp.int32, (1, 128), 1)

    def pick(row, k):
        return jnp.sum(jnp.where(lane == k, row, 0.0), axis=1, keepdims=True)

    def put(k, value):
        return jnp.where(lane == k, value, 0.0)

    eye_16 = lax.broadcasted_iota(jnp.int32, (16, 16), 0) == lax.broadcasted_iota(
        jnp.int32, (16, 16), 1
    )
    lane_16 = lax.broadcasted_iota(jnp.int32, (16, 128), 1).astype(F32)
    for q in range(8):
        column = jnp.sum(
            jnp.where(eye_16, map_ref[q : q + 1, :].astype(F32), 0.0), axis=1, keepdims=True
        )
        mcol[q] = jnp.where(lane_16 == column, 1.0, 0.0)
    cscr[...] = jnp.zeros_like(cscr)
    cscr[:, :64] = cinv_ref[0]

    def restrict(x):
        row = jnp.zeros((1, 128), F32)
        for q in range(8):
            acc = x[:16] * corner_ref[q : q + 1, :128]
            for k in range(1, 4):
                acc += x[16 * k : 16 * (k + 1)] * corner_ref[q : q + 1, 128 * k : 128 * (k + 1)]
            vertex = jnp.sum(acc, axis=1, keepdims=True)
            row += jnp.sum(vertex * mcol[q], axis=0, keepdims=True)
        return row

    eye_64 = lax.broadcasted_iota(jnp.int32, (64, 128), 0) == lax.broadcasted_iota(
        jnp.int32, (64, 128), 1
    )

    def solve(coarse):
        column = jnp.sum(jnp.where(eye_64, coarse, 0.0), axis=1, keepdims=True)
        return jnp.sum(cscr[...] * column, axis=0, keepdims=True)

    def prolong(solved):
        blocks = [jnp.zeros((16, 128), F32) for _ in range(4)]
        for q in range(8):
            at_vertex = jnp.sum(mcol[q] * solved, axis=1, keepdims=True)
            for k in range(4):
                blocks[k] += at_vertex * corner_ref[q : q + 1, 128 * k : 128 * (k + 1)]
        return jnp.concatenate(blocks, axis=0)

    def copy_sub(src, dst, sem, peer):
        return pltpu.make_async_remote_copy(
            src_ref=src,
            dst_ref=dst,
            send_sem=send_sem.at[sem],
            recv_sem=recv_sem.at[sem],
            device_id={"sub": peer},
            device_id_type=MESH,
        )

    def copy_grp(src, dst, sem, peer):
        return pltpu.make_async_remote_copy(
            src_ref=src,
            dst_ref=dst,
            send_sem=send_sem.at[sem],
            recv_sem=recv_sem.at[sem],
            device_id={"grp": peer},
            device_id_type=MESH,
        )

    def wait_bytes(ref, sem):
        pltpu.make_async_copy(ref, ref, sem).wait()

    def sum_sub_start(phase, row):
        send_r[phase] = row
        recv_r[phase, s] = row

        def go(k, carry):
            peer = lax.rem(s + k, ns)
            copy_sub(send_r.at[phase], recv_r.at[phase, s], 12 + phase, peer).start()
            return carry

        lax.fori_loop(1, ns, go, 0, unroll=True)

    def sum_sub(phase):
        wait_bytes(recv_r.at[phase, pl.ds(0, ns - 1)], recv_sem.at[12 + phase])
        return jnp.sum(recv_r[phase], axis=0)

    def sum_grp_start(phase, row):
        send_b[phase] = row
        recv_b[phase, g] = row

        def go(k, carry):
            peer = lax.rem(g + k, ng)
            copy_grp(send_b.at[phase], recv_b.at[phase, g], 16 + phase, peer).start()
            return carry

        lax.fori_loop(1, ng, go, 0, unroll=True)

    def sum_grp(phase):
        wait_bytes(recv_b.at[phase, pl.ds(0, ng - 1)], recv_sem.at[16 + phase])
        return jnp.sum(recv_b[phase], axis=0)

    residual = cube(right_ref)
    partial_coarse = restrict(residual)

    idx[:ns, :] = slots_ref[0]
    for k in range(2):
        for m in range(FACE):
            at = ns + FACE * k + m
            idx[at : at + 1, :] = face_ref[k : k + 1, 128 * m : 128 * (m + 1)]
        for m in range(PAIR):
            at = at_pair + PAIR * k + m
            idx[at : at + 1, :] = pair_ref[k : k + 1, 128 * m : 128 * (m + 1)]
    points = idx[...]
    row_of = ((points >> 7) & 3) * 16 + (points >> 9)
    hi_ref[...] = jnp.where(points >= 8192, 1024, row_of)
    lo_ref[...] = points & 127

    def gather(first, last):
        high = hi_ref[first:last, :]
        low = lo_ref[first:last, :]

        def step(t, acc):
            block = x_ref[pl.ds(pl.multiple_of(t * 8, 8), 8), :]
            for r in range(8):
                row = jnp.broadcast_to(block[r : r + 1], (last - first, 128))
                got = jnp.take_along_axis(row, low, axis=1, mode="promise_in_bounds")
                acc = jnp.where(high == t * 8 + r, got, acc)
            return acc

        return lax.fori_loop(
            0, 8, step, jnp.zeros((last - first, 128), F32), unroll=True
        )

    def look(table, at):
        return jnp.take_along_axis(table, at, axis=1, mode="promise_in_bounds")

    map_scr[...] = jnp.zeros_like(map_scr)
    map_scr[:, :16] = map_ref[...]
    lane_8 = lax.broadcasted_iota(jnp.int32, (8, 128), 1)
    corner_row = lax.broadcasted_iota(jnp.int32, (8, 128), 0) == lane_8 >> 4
    spread = look(map_scr[...], lane_8 & 15).astype(F32)
    map_row = jnp.sum(jnp.where(corner_row, spread, 0.0), axis=0, keepdims=True)
    x_ref[...] = cube(jac_ref) * residual
    send_h[:, :, :128] = jnp.broadcast_to(partial_coarse.reshape(1, 1, 128), (ns, 1, 128))
    send_h[:, :, 128:] = gather(0, ns).reshape(ns, 1, 128)
    send_t[:, :, :128] = jnp.broadcast_to(
        map_row.astype(jnp.int32).reshape(1, 1, 128), (ns, 1, 128)
    )
    send_t[:, :, 128:] = points[:ns].reshape(ns, 1, 128)
    recv_h[s, :, :128] = partial_coarse

    pl.semaphore_wait(barrier, ns + ng - 2)

    def hello(k, carry):
        peer = lax.rem(s + k, ns)
        copy_sub(send_h.at[peer], recv_h.at[s], 18, peer).start()
        copy_sub(send_t.at[peer], recv_t.at[s], 19, peer).start()
        return carry

    lax.fori_loop(1, ns, hello, 0, unroll=True)

    sub_128 = lax.broadcasted_iota(jnp.int32, (128, 128), 0)
    sub_64 = lax.broadcasted_iota(jnp.int32, (64, 128), 0)

    def build(t, carry):
        low = lo_ref[pl.ds(pl.multiple_of(t * 8, 8), 8), :]
        ohlo[t] = jnp.concatenate(
            [jnp.where(sub_128 == low[r : r + 1], 1.0, 0.0).astype(BF16) for r in range(8)],
            axis=1,
        )
        return carry

    lax.fori_loop(0, tiles, build, 0, unroll=True)

    def scatter(first, last, acc):
        def step(t, acc):
            at = pl.ds(pl.multiple_of(t * 8, 8), 8)
            high = hi_ref[at, :]
            value = val_ref[at, :]
            upper = value.astype(BF16).astype(F32)
            lower = value - upper
            parts = []
            for r in range(8):
                hit = sub_64 == high[r : r + 1]
                parts.append(
                    jnp.concatenate(
                        [
                            jnp.where(hit, upper[r : r + 1], 0.0),
                            jnp.where(hit, lower[r : r + 1], 0.0),
                        ],
                        axis=0,
                    ).astype(BF16)
                )
            left = jnp.concatenate(parts, axis=1)
            return acc + lax.dot_general(
                left, ohlo[t], (((1,), (1,)), ((), ())), preferred_element_type=F32
            )

        return lax.fori_loop(first, last, step, acc, unroll=True)

    def send_slots(phase):
        send_s[phase] = gather(0, ns).reshape(ns, 1, 128)

        def go(k, carry):
            peer = lax.rem(s + k, ns)
            copy_sub(send_s.at[phase, peer], recv_s.at[phase, s], phase, peer).start()
            return carry

        lax.fori_loop(1, ns, go, 0, unroll=True)

    def send_faces(phase):
        got = gather(ns, at_pair)
        send_f[phase, 0] = got[:FACE]
        send_f[phase, 1] = got[FACE:]
        down = copy_grp(send_f.at[phase, 0], recv_f.at[phase, 1], 4 + phase, prv)
        up = copy_grp(send_f.at[phase, 1], recv_f.at[phase, 0], 8 + phase, nxt)
        down.start()
        up.start()
        return down, up

    def add_pairs():
        got = gather(at_pair, rows)
        val_ref[at_pair : at_pair + PAIR, :] = got[PAIR:]
        val_ref[at_pair + PAIR :, :] = got[:PAIR]
        return scatter(at_pair // 8, tiles, jnp.zeros((128, 128), F32))

    def add_faces(phase, copies, acc):
        for copy in copies:
            copy.wait_recv()
        val_ref[ns : ns + FACE, :] = jnp.where(g == 0, 0.0, recv_f[phase, 0])
        val_ref[ns + FACE : at_pair, :] = jnp.where(g == ng - 1, 0.0, recv_f[phase, 1])
        return scatter(ns // 8, at_pair // 8, acc)

    def wait_slots(phase):
        wait_bytes(recv_s.at[phase, pl.ds(0, ns - 1)], recv_sem.at[phase])
        return recv_s[phase].reshape(ns, 128)

    def add_slots(value, acc):
        val_ref[:ns, :] = value
        return scatter(0, ns // 8, acc)

    def assemble(phase, x, meanwhile=lambda: None, before_slots=lambda: None):
        x_ref[...] = x
        send_slots(phase)
        copies = send_faces(phase)
        meanwhile()
        acc = add_faces(phase, copies, add_pairs())
        before_slots()
        acc = add_slots(wait_slots(phase), acc)
        return x + acc[:64] + acc[64:]

    def assemble_known(phase, x, slot_values):
        x_ref[...] = x
        copies = send_faces(phase)
        acc = add_slots(slot_values, add_pairs())
        acc = add_faces(phase, copies, acc)
        return x + acc[:64] + acc[64:]

    def peer_points():
        return recv_t[:, :, 128:].reshape(ns, 128)

    def corner_functions():
        point = peer_points()
        table = jnp.broadcast_to(corner_ref[8:9, :128], (ns, 128))
        nodes = [(point >> 6) & 7, (point >> 3) & 7, point & 7]
        near = [[look(table, node + 8 * bit) for bit in range(2)] for node in nodes]
        for q in range(8):
            phi[q] = near[0][q >> 2 & 1] * near[1][q >> 1 & 1] * near[2][q & 1]

    def coarse_at_peers(solved):
        corners = look(jnp.broadcast_to(solved, (ns, 128)), recv_t[:, :, :128].reshape(ns, 128))
        element = (peer_points() >> 9) & 15
        out = jnp.zeros((ns, 128), F32)
        for q in range(8):
            out += phi[q] * look(corners, element + 16 * q)
        return out

    def split(x):
        upper = x.astype(BF16)
        return upper, (x - upper.astype(F32)).astype(BF16)

    def dot(a, b):
        return jnp.dot(a, b, preferred_element_type=F32)

    def dot_right(x, k):
        upper, lower = split(x)
        both = dot(jnp.concatenate([upper, lower], axis=0), mats_ref[k])
        return both[:64] + both[64:] + dot(upper, mats_ref[k + 6])

    left_half = lax.broadcasted_iota(jnp.int32, (64, 128), 1) < 64

    def dot_rows(x, k):
        upper, lower = split(jnp.concatenate([x, pltpu.roll(x, 64, 1)], axis=0))
        both = dot(mats_ref[k], jnp.concatenate([upper, lower], axis=1))
        out = both[:, :128] + both[:, 128:] + dot(mats_ref[k + 6], upper)
        return jnp.where(left_half, out[:64], out[64:])

    def stiffness(x):
        flux_first = cube(metric_ref, 0) * dot_rows(x, 4)
        flux_second = cube(metric_ref, 512) * dot_right(x, 0)
        flux_third = cube(metric_ref, 1024) * dot_right(x, 1)
        return dot_rows(flux_first, 5) + dot_right(flux_second, 2) + dot_right(flux_third, 3)

    right = residual
    part = cube(jac_ref) * right
    wait_bytes(recv_t.at[pl.ds(0, ns - 1)], recv_sem.at[19])
    corner_functions()
    wait_bytes(recv_h.at[pl.ds(0, ns - 1)], recv_sem.at[18])
    solved = solve(jnp.sum(recv_h[:, :, :128], axis=0))
    first = part + prolong(solved)
    summed = assemble_known(
        0, first, recv_h[:, :, 128:].reshape(ns, 128) + coarse_at_peers(solved)
    )
    inner = stiffness(summed)
    mass = cube(helm_ref) * first

    def first_sums():
        row = put(0, total(right * first)) + put(1, total(summed * inner + first * mass))
        sum_sub_start(1, row)

    image = assemble(1, inner, first_sums)
    image += mass
    sum_sub_start(2, restrict(image))
    part = cube(jac_ref) * image
    x_ref[...] = part
    send_slots(2)
    sum_grp_start(0, sum_sub(1))
    solved = solve(sum_sub(2))
    second = part + prolong(solved)
    known = coarse_at_peers(solved)
    summed_second = assemble_known(2, second, wait_slots(2) + known)
    inner_second = stiffness(summed_second)
    sums = sum_grp(0)
    rz_first, curved = pick(sums, 0), pick(sums, 1)
    alpha = rz_first / curved
    residual = right - alpha * image
    smoothed = first - alpha * second
    row = (
        put(0, total(residual * smoothed))
        + put(1, total(smoothed * image))
        + put(
            2,
            total(
                (summed - alpha * summed_second) * (inner - alpha * inner_second)
                + smoothed * (cube(helm_ref) * smoothed)
            ),
        )
    )
    sum_sub_start(3, row)

    def last_sums():
        sum_grp_start(1, sum_sub(3))

    image_second = assemble(3, inner_second, before_slots=last_sums)
    image_second += cube(helm_ref) * second
    sums = sum_grp(1)
    rz_second = pick(sums, 0)
    beta = rz_second / rz_first
    curve = pick(sums, 2) + 2.0 * beta * pick(sums, 1) + beta * beta * curved
    alpha_last = rz_second / curve
    solved = alpha * first + alpha_last * (smoothed + beta * first)
    residual = residual - alpha_last * (image - alpha * image_second + beta * image)
    for k in range(4):
        sol_ref[:, 128 * k : 128 * (k + 1)] = solved[16 * k : 16 * (k + 1)]
        res_ref[:, 128 * k : 128 * (k + 1)] = residual[16 * k : 16 * (k + 1)]

    for phase in range(1, 4):
        wait_bytes(send_s.at[phase, pl.ds(0, ns - 1)], send_sem.at[phase])
    for phase in range(4):
        wait_bytes(send_f.at[phase, 0], send_sem.at[4 + phase])
        wait_bytes(send_f.at[phase, 1], send_sem.at[8 + phase])
    wait_bytes(send_h.at[pl.ds(0, ns - 1)], send_sem.at[18])
    wait_bytes(send_t.at[pl.ds(0, ns - 1)], send_sem.at[19])
    for phase in range(1, 4):
        wait_bytes(recv_r.at[phase, pl.ds(0, ns - 1)], send_sem.at[12 + phase])
    for phase in range(2):
        wait_bytes(recv_b.at[phase, pl.ds(0, ng - 1)], send_sem.at[16 + phase])


def body(ns, ng, *args):
    mats, corner = tables()
    rows = 2 * PAIR + ns + 2 * FACE
    vmem = pl.BlockSpec(memory_space=pltpu.VMEM)
    shape = jax.ShapeDtypeStruct((16, 512), F32)
    return pl.pallas_call(
        functools.partial(kernel, ns, ng),
        out_shape=(shape, shape),
        in_specs=[vmem] * 11,
        out_specs=(vmem, vmem),
        scratch_shapes=[
            pltpu.VMEM((rows, 128), jnp.int32),
            pltpu.VMEM((rows, 128), jnp.int32),
            pltpu.VMEM((rows, 128), jnp.int32),
            pltpu.VMEM((rows // 8, 128, 1024), BF16),
            pltpu.VMEM((64, 128), F32),
            pltpu.VMEM((rows, 128), F32),
            pltpu.VMEM((64, 128), F32),
            pltpu.VMEM((8, 16, 128), F32),
            pltpu.VMEM((4, ns, 1, 128), F32),
            pltpu.VMEM((4, ns, 1, 128), F32),
            pltpu.VMEM((4, 2, FACE, 128), F32),
            pltpu.VMEM((4, 2, FACE, 128), F32),
            pltpu.VMEM((4, 1, 128), F32),
            pltpu.VMEM((4, ns, 1, 128), F32),
            pltpu.VMEM((2, 1, 128), F32),
            pltpu.VMEM((2, ng, 1, 128), F32),
            pltpu.VMEM((ns, 1, 256), F32),
            pltpu.VMEM((ns, 1, 256), F32),
            pltpu.VMEM((ns, 1, 256), jnp.int32),
            pltpu.VMEM((ns, 1, 256), jnp.int32),
            pltpu.VMEM((8, 128), jnp.int32),
            pltpu.VMEM((8, ns, 128), F32),
            pltpu.SemaphoreType.DMA((20,)),
            pltpu.SemaphoreType.DMA((20,)),
        ],
        compiler_params=pltpu.CompilerParams(collective_id=0, has_side_effects=True),
    )(*args, mats, corner)


def solution(mesh):
    in_specs = (
        P(("grp", "sub"), None),
        P(("grp", "sub"), None),
        P(("grp", "sub"), None),
        P(("grp", "sub"), None),
        P(None, ("grp", "sub")),
        P(("grp", "sub"), None, None),
        P(None, ("grp", "sub")),
        P(None, ("grp", "sub")),
        P("grp", None, None),
    )
    out_specs = (P(("grp", "sub"), None), P(("grp", "sub"), None))
    return jax.shard_map(
        functools.partial(body, mesh.shape["sub"], mesh.shape["grp"]),
        mesh=mesh,
        in_specs=in_specs,
        out_specs=out_specs,
        check_vma=False,
    )
```

```python
import functools

import jax
import jax.numpy as jnp
import numpy as np
from jax import lax
from jax.experimental import pallas as pl
from jax.experimental.pallas import tpu as pltpu
from jax.sharding import PartitionSpec as P

MESH = pl.DeviceIdType.MESH
F32 = jnp.float32
BF16 = jnp.bfloat16
PAIR = 8
FACE = 4


def tables():
    order_index = np.arange(8)
    colloc = np.cos(np.pi * order_index / 7.0)
    end_weights = (
        np.where((order_index == 0) | (order_index == 7), 2.0, 1.0) * (-1.0) ** order_index
    )
    spacing = colloc[:, None] - colloc[None, :] + np.eye(8)
    raw_matrix = np.outer(end_weights, 1.0 / end_weights) / spacing
    off_part = raw_matrix * (1.0 - np.eye(8))
    derivative = 0.25 * (off_part - np.eye(8) * off_part.sum(axis=1)[:, None])
    derivative = derivative.astype(np.float32).astype(np.float64)
    eye2, eye8, eye16 = np.eye(2), np.eye(8), np.eye(16)

    def rows_matrix(mat):
        def part(out_low, in_low):
            return np.kron(mat[out_low::2, in_low::2], eye16)

        return np.block([[part(0, 0), part(0, 1)], [part(1, 1), part(1, 0)]])

    along_second = np.kron(eye2, np.kron(derivative, eye8)).T
    along_third = np.kron(eye16, derivative).T
    stack = [
        along_second,
        along_third,
        along_second.T,
        along_third.T,
        rows_matrix(derivative),
        rows_matrix(derivative.T),
    ]
    high = [np.asarray(m, np.float32).astype(jnp.bfloat16) for m in stack]
    low = [
        (np.asarray(m, np.float32) - h.astype(np.float32)).astype(jnp.bfloat16)
        for m, h in zip(stack, high)
    ]
    mats = np.stack(high + low)
    point_index = np.arange(512)
    corner_index = np.arange(8)
    sign_first = 1.0 - 2.0 * (corner_index >> 2 & 1)
    sign_second = 1.0 - 2.0 * (corner_index >> 1 & 1)
    sign_third = 1.0 - 2.0 * (corner_index & 1)
    node_first = colloc[point_index // 64][:, None]
    node_second = colloc[point_index // 8 % 8][:, None]
    node_third = colloc[point_index % 8][:, None]
    corner = (
        0.5
        * (1.0 + sign_first[None, :] * node_first)
        * (0.5 * (1.0 + sign_second[None, :] * node_second))
        * (0.5 * (1.0 + sign_third[None, :] * node_third))
    )
    factors = np.zeros((8, 512))
    factors[0, :8] = 0.5 * (1.0 + colloc)
    factors[0, 8:16] = 0.5 * (1.0 - colloc)
    return jnp.asarray(mats), jnp.asarray(np.concatenate([corner.T, factors]), F32)


def kernel(
    ns,
    ng,
    right_ref,
    metric_ref,
    helm_ref,
    jac_ref,
    pair_ref,
    slots_ref,
    face_ref,
    map_ref,
    cinv_ref,
    mats_ref,
    corner_ref,
    out_ref,
    idx,
    hi_ref,
    lo_ref,
    ohlo,
    x_ref,
    val_ref,
    cscr,
    mcol,
    send_s,
    recv_s,
    send_f,
    recv_f,
    send_r,
    recv_r,
    send_b,
    recv_b,
    send_h,
    recv_h,
    send_t,
    recv_t,
    map_scr,
    phi,
    send_sem,
    recv_sem,
):
    g = lax.axis_index("grp")
    s = lax.axis_index("sub")
    nxt, prv = lax.rem(g + 1, ng), lax.rem(g + ng - 1, ng)
    rows = 2 * PAIR + ns + 2 * FACE
    tiles = rows // 8
    at_pair = ns + 2 * FACE

    recv_s[...] = jnp.zeros_like(recv_s)
    recv_h[...] = jnp.zeros_like(recv_h)
    recv_t[...] = jnp.zeros_like(recv_t)

    barrier = pltpu.get_barrier_semaphore()

    def greet_sub(k, carry):
        pl.semaphore_signal(
            barrier, inc=1, device_id={"sub": lax.rem(s + k, ns)}, device_id_type=MESH
        )
        return carry

    def greet_grp(k, carry):
        pl.semaphore_signal(
            barrier, inc=1, device_id={"grp": lax.rem(g + k, ng)}, device_id_type=MESH
        )
        return carry

    lax.fori_loop(1, ns, greet_sub, 0, unroll=True)
    lax.fori_loop(1, ng, greet_grp, 0, unroll=True)

    def cube(ref, base=0):
        return jnp.concatenate(
            [ref[:, base + 128 * k : base + 128 * (k + 1)] for k in range(4)], axis=0
        )

    def total(x):
        return jnp.sum(jnp.sum(x, axis=0, keepdims=True), axis=1, keepdims=True)

    lane = lax.broadcasted_iota(jnp.int32, (1, 128), 1)

    def pick(row, k):
        return jnp.sum(jnp.where(lane == k, row, 0.0), axis=1, keepdims=True)

    def put(k, value):
        return jnp.where(lane == k, value, 0.0)

    eye_16 = lax.broadcasted_iota(jnp.int32, (16, 16), 0) == lax.broadcasted_iota(
        jnp.int32, (16, 16), 1
    )
    lane_16 = lax.broadcasted_iota(jnp.int32, (16, 128), 1).astype(F32)
    for q in range(8):
        column = jnp.sum(
            jnp.where(eye_16, map_ref[q : q + 1, :].astype(F32), 0.0), axis=1, keepdims=True
        )
        mcol[q] = jnp.where(lane_16 == column, 1.0, 0.0)
    cscr[...] = jnp.zeros_like(cscr)
    cscr[:, :64] = cinv_ref[0]

    def restrict(x):
        row = jnp.zeros((1, 128), F32)
        for q in range(8):
            acc = x[:16] * corner_ref[q : q + 1, :128]
            for k in range(1, 4):
                acc += x[16 * k : 16 * (k + 1)] * corner_ref[q : q + 1, 128 * k : 128 * (k + 1)]
            vertex = jnp.sum(acc, axis=1, keepdims=True)
            row += jnp.sum(vertex * mcol[q], axis=0, keepdims=True)
        return row

    eye_64 = lax.broadcasted_iota(jnp.int32, (64, 128), 0) == lax.broadcasted_iota(
        jnp.int32, (64, 128), 1
    )

    def solve(coarse):
        column = jnp.sum(jnp.where(eye_64, coarse, 0.0), axis=1, keepdims=True)
        return jnp.sum(cscr[...] * column, axis=0, keepdims=True)

    def prolong(solved):
        blocks = [jnp.zeros((16, 128), F32) for _ in range(4)]
        for q in range(8):
            at_vertex = jnp.sum(mcol[q] * solved, axis=1, keepdims=True)
            for k in range(4):
                blocks[k] += at_vertex * corner_ref[q : q + 1, 128 * k : 128 * (k + 1)]
        return jnp.concatenate(blocks, axis=0)

    def copy_sub(src, dst, sem, peer):
        return pltpu.make_async_remote_copy(
            src_ref=src,
            dst_ref=dst,
            send_sem=send_sem.at[sem],
            recv_sem=recv_sem.at[sem],
            device_id={"sub": peer},
            device_id_type=MESH,
        )

    def copy_grp(src, dst, sem, peer):
        return pltpu.make_async_remote_copy(
            src_ref=src,
            dst_ref=dst,
            send_sem=send_sem.at[sem],
            recv_sem=recv_sem.at[sem],
            device_id={"grp": peer},
            device_id_type=MESH,
        )

    def wait_bytes(ref, sem):
        pltpu.make_async_copy(ref, ref, sem).wait()

    def sum_sub_start(phase, row):
        send_r[phase] = row
        recv_r[phase, s] = row

        def go(k, carry):
            peer = lax.rem(s + k, ns)
            copy_sub(send_r.at[phase], recv_r.at[phase, s], 12 + phase, peer).start()
            return carry

        lax.fori_loop(1, ns, go, 0, unroll=True)

    def sum_sub(phase):
        wait_bytes(recv_r.at[phase, pl.ds(0, ns - 1)], recv_sem.at[12 + phase])
        return jnp.sum(recv_r[phase], axis=0)

    def sum_grp_start(phase, row):
        send_b[phase] = row
        recv_b[phase, g] = row

        def go(k, carry):
            peer = lax.rem(g + k, ng)
            copy_grp(send_b.at[phase], recv_b.at[phase, g], 16 + phase, peer).start()
            return carry

        lax.fori_loop(1, ng, go, 0, unroll=True)

    def sum_grp(phase):
        wait_bytes(recv_b.at[phase, pl.ds(0, ng - 1)], recv_sem.at[16 + phase])
        return jnp.sum(recv_b[phase], axis=0)

    residual = cube(right_ref)
    partial_coarse = restrict(residual)

    idx[:ns, :] = slots_ref[0]
    for k in range(2):
        for m in range(FACE):
            at = ns + FACE * k + m
            idx[at : at + 1, :] = face_ref[k : k + 1, 128 * m : 128 * (m + 1)]
        for m in range(PAIR):
            at = at_pair + PAIR * k + m
            idx[at : at + 1, :] = pair_ref[k : k + 1, 128 * m : 128 * (m + 1)]
    points = idx[...]
    row_of = ((points >> 7) & 3) * 16 + (points >> 9)
    hi_ref[...] = jnp.where(points >= 8192, 1024, row_of)
    lo_ref[...] = points & 127

    def gather(first, last):
        high = hi_ref[first:last, :]
        low = lo_ref[first:last, :]

        def step(t, acc):
            block = x_ref[pl.ds(pl.multiple_of(t * 8, 8), 8), :]
            for r in range(8):
                row = jnp.broadcast_to(block[r : r + 1], (last - first, 128))
                got = jnp.take_along_axis(row, low, axis=1, mode="promise_in_bounds")
                acc = jnp.where(high == t * 8 + r, got, acc)
            return acc

        return lax.fori_loop(
            0, 8, step, jnp.zeros((last - first, 128), F32), unroll=True
        )

    def look(table, at):
        return jnp.take_along_axis(table, at, axis=1, mode="promise_in_bounds")

    map_scr[...] = jnp.zeros_like(map_scr)
    map_scr[:, :16] = map_ref[...]
    lane_8 = lax.broadcasted_iota(jnp.int32, (8, 128), 1)
    corner_row = lax.broadcasted_iota(jnp.int32, (8, 128), 0) == lane_8 >> 4
    spread = look(map_scr[...], lane_8 & 15).astype(F32)
    map_row = jnp.sum(jnp.where(corner_row, spread, 0.0), axis=0, keepdims=True)
    x_ref[...] = cube(jac_ref) * residual
    send_h[:, :, :128] = jnp.broadcast_to(partial_coarse.reshape(1, 1, 128), (ns, 1, 128))
    send_h[:, :, 128:] = gather(0, ns).reshape(ns, 1, 128)
    send_t[:, :, :128] = jnp.broadcast_to(
        map_row.astype(jnp.int32).reshape(1, 1, 128), (ns, 1, 128)
    )
    send_t[:, :, 128:] = points[:ns].reshape(ns, 1, 128)
    recv_h[s, :, :128] = partial_coarse

    pl.semaphore_wait(barrier, ns + ng - 2)

    def hello(k, carry):
        peer = lax.rem(s + k, ns)
        copy_sub(send_h.at[peer], recv_h.at[s], 18, peer).start()
        return carry

    def hello_tables(k, carry):
        peer = lax.rem(s + k, ns)
        copy_sub(send_t.at[peer], recv_t.at[s], 19, peer).start()
        return carry

    lax.fori_loop(1, ns, hello, 0, unroll=True)
    lax.fori_loop(1, ns, hello_tables, 0, unroll=True)

    sub_128 = lax.broadcasted_iota(jnp.int32, (128, 128), 0)
    sub_64 = lax.broadcasted_iota(jnp.int32, (64, 128), 0)

    def build(t, carry):
        low = lo_ref[pl.ds(pl.multiple_of(t * 8, 8), 8), :]
        ohlo[t] = jnp.concatenate(
            [jnp.where(sub_128 == low[r : r + 1], 1.0, 0.0).astype(BF16) for r in range(8)],
            axis=1,
        )
        return carry

    lax.fori_loop(0, tiles, build, 0, unroll=True)

    def scatter(first, last, acc):
        def step(t, acc):
            at = pl.ds(pl.multiple_of(t * 8, 8), 8)
            high = hi_ref[at, :]
            value = val_ref[at, :]
            upper = value.astype(BF16).astype(F32)
            lower = value - upper
            parts = []
            for r in range(8):
                hit = sub_64 == high[r : r + 1]
                parts.append(
                    jnp.concatenate(
                        [
                            jnp.where(hit, upper[r : r + 1], 0.0),
                            jnp.where(hit, lower[r : r + 1], 0.0),
                        ],
                        axis=0,
                    ).astype(BF16)
                )
            left = jnp.concatenate(parts, axis=1)
            return acc + lax.dot_general(
                left, ohlo[t], (((1,), (1,)), ((), ())), preferred_element_type=F32
            )

        return lax.fori_loop(first, last, step, acc, unroll=True)

    def send_slots(phase):
        send_s[phase] = gather(0, ns).reshape(ns, 1, 128)

        def go(k, carry):
            peer = lax.rem(s + k, ns)
            copy_sub(send_s.at[phase, peer], recv_s.at[phase, s], phase, peer).start()
            return carry

        lax.fori_loop(1, ns, go, 0, unroll=True)

    def send_faces(phase):
        got = gather(ns, at_pair)
        send_f[phase, 0] = got[:FACE]
        send_f[phase, 1] = got[FACE:]
        down = copy_grp(send_f.at[phase, 0], recv_f.at[phase, 1], 4 + phase, prv)
        up = copy_grp(send_f.at[phase, 1], recv_f.at[phase, 0], 8 + phase, nxt)
        down.start()
        up.start()
        return down, up

    def add_pairs():
        got = gather(at_pair, rows)
        val_ref[at_pair : at_pair + PAIR, :] = got[PAIR:]
        val_ref[at_pair + PAIR :, :] = got[:PAIR]
        return scatter(at_pair // 8, tiles, jnp.zeros((128, 128), F32))

    def add_faces(phase, copies, acc):
        for copy in copies:
            copy.wait_recv()
        val_ref[ns : ns + FACE, :] = jnp.where(g == 0, 0.0, recv_f[phase, 0])
        val_ref[ns + FACE : at_pair, :] = jnp.where(g == ng - 1, 0.0, recv_f[phase, 1])
        return scatter(ns // 8, at_pair // 8, acc)

    def wait_slots(phase):
        wait_bytes(recv_s.at[phase, pl.ds(0, ns - 1)], recv_sem.at[phase])
        return recv_s[phase].reshape(ns, 128)

    def add_slots(value, acc):
        val_ref[:ns, :] = value
        return scatter(0, ns // 8, acc)

    def assemble(phase, x, meanwhile=lambda: None, before_slots=lambda: None):
        x_ref[...] = x
        send_slots(phase)
        copies = send_faces(phase)
        meanwhile()
        acc = add_faces(phase, copies, add_pairs())
        before_slots()
        acc = add_slots(wait_slots(phase), acc)
        return x + acc[:64] + acc[64:]

    def assemble_known(phase, x, slot_values):
        x_ref[...] = x
        copies = send_faces(phase)
        acc = add_pairs()
        acc = add_slots(slot_values(), acc)
        acc = add_faces(phase, copies, acc)
        return x + acc[:64] + acc[64:]

    def peer_points():
        return recv_t[:, :, 128:].reshape(ns, 128)

    def corner_functions():
        point = peer_points()
        table = jnp.broadcast_to(corner_ref[8:9, :128], (ns, 128))
        nodes = [(point >> 6) & 7, (point >> 3) & 7, point & 7]
        near = [[look(table, node + 8 * bit) for bit in range(2)] for node in nodes]
        for q in range(8):
            phi[q] = near[0][q >> 2 & 1] * near[1][q >> 1 & 1] * near[2][q & 1]

    def coarse_at_peers(solved):
        corners = look(jnp.broadcast_to(solved, (ns, 128)), recv_t[:, :, :128].reshape(ns, 128))
        element = (peer_points() >> 9) & 15
        out = jnp.zeros((ns, 128), F32)
        for q in range(8):
            out += phi[q] * look(corners, element + 16 * q)
        return out

    def split(x):
        upper = x.astype(BF16)
        return upper, (x - upper.astype(F32)).astype(BF16)

    def dot(a, b):
        return jnp.dot(a, b, preferred_element_type=F32)

    def dot_right(x, k):
        upper, lower = split(x)
        both = dot(jnp.concatenate([upper, lower], axis=0), mats_ref[k])
        return both[:64] + both[64:] + dot(upper, mats_ref[k + 6])

    left_half = lax.broadcasted_iota(jnp.int32, (64, 128), 1) < 64

    def dot_rows(x, k):
        upper, lower = split(jnp.concatenate([x, pltpu.roll(x, 64, 1)], axis=0))
        both = dot(mats_ref[k], jnp.concatenate([upper, lower], axis=1))
        out = both[:, :128] + both[:, 128:] + dot(mats_ref[k + 6], upper)
        return jnp.where(left_half, out[:64], out[64:])

    def stiffness(x):
        flux_first = cube(metric_ref, 0) * dot_rows(x, 4)
        flux_second = cube(metric_ref, 512) * dot_right(x, 0)
        flux_third = cube(metric_ref, 1024) * dot_right(x, 1)
        return dot_rows(flux_first, 5) + dot_right(flux_second, 2) + dot_right(flux_third, 3)

    right = residual
    part = cube(jac_ref) * right
    wait_bytes(recv_h.at[pl.ds(0, ns - 1)], recv_sem.at[18])
    solved = solve(jnp.sum(recv_h[:, :, :128], axis=0))
    first = part + prolong(solved)

    def first_slots():
        wait_bytes(recv_t.at[pl.ds(0, ns - 1)], recv_sem.at[19])
        corner_functions()
        return recv_h[:, :, 128:].reshape(ns, 128) + coarse_at_peers(solved)

    summed = assemble_known(0, first, first_slots)
    inner = stiffness(summed)
    mass = cube(helm_ref) * first

    def first_sums():
        row = put(0, total(right * first)) + put(1, total(summed * inner + first * mass))
        sum_sub_start(1, row)

    image = assemble(1, inner, first_sums)
    image += mass
    sum_sub_start(2, restrict(image))
    part = cube(jac_ref) * image
    x_ref[...] = part
    send_slots(2)
    sum_grp_start(0, sum_sub(1))
    solved_second = solve(sum_sub(2))
    second = part + prolong(solved_second)

    def second_slots():
        known = coarse_at_peers(solved_second)
        return wait_slots(2) + known

    summed_second = assemble_known(2, second, second_slots)
    inner_second = stiffness(summed_second)
    sums = sum_grp(0)
    rz_first, curved = pick(sums, 0), pick(sums, 1)
    alpha = rz_first / curved
    residual = right - alpha * image
    smoothed = first - alpha * second
    row = (
        put(0, total(residual * smoothed))
        + put(1, total(smoothed * image))
        + put(
            2,
            total(
                (summed - alpha * summed_second) * (inner - alpha * inner_second)
                + smoothed * (cube(helm_ref) * smoothed)
            ),
        )
    )
    sum_sub_start(3, row)

    def last_sums():
        sum_grp_start(1, sum_sub(3))

    image_second = assemble(3, inner_second, before_slots=last_sums)
    image_second += cube(helm_ref) * second
    sums = sum_grp(1)
    rz_second = pick(sums, 0)
    beta = rz_second / rz_first
    curve = pick(sums, 2) + 2.0 * beta * pick(sums, 1) + beta * beta * curved
    alpha_last = rz_second / curve
    solved = alpha * first + alpha_last * (smoothed + beta * first)
    residual = residual - alpha_last * (image - alpha * image_second + beta * image)
    for k in range(4):
        out_ref[0, :, 128 * k : 128 * (k + 1)] = solved[16 * k : 16 * (k + 1)]
        out_ref[1, :, 128 * k : 128 * (k + 1)] = residual[16 * k : 16 * (k + 1)]

    for phase in range(1, 4):
        wait_bytes(send_s.at[phase, pl.ds(0, ns - 1)], send_sem.at[phase])
    for phase in range(4):
        wait_bytes(send_f.at[phase, 0], send_sem.at[4 + phase])
        wait_bytes(send_f.at[phase, 1], send_sem.at[8 + phase])
    wait_bytes(send_h.at[pl.ds(0, ns - 1)], send_sem.at[18])
    wait_bytes(send_t.at[pl.ds(0, ns - 1)], send_sem.at[19])
    for phase in range(1, 4):
        wait_bytes(recv_r.at[phase, pl.ds(0, ns - 1)], send_sem.at[12 + phase])
    for phase in range(2):
        wait_bytes(recv_b.at[phase, pl.ds(0, ng - 1)], send_sem.at[16 + phase])


def body(ns, ng, *args):
    mats, corner = tables()
    rows = 2 * PAIR + ns + 2 * FACE
    vmem = pl.BlockSpec(memory_space=pltpu.VMEM)
    shape = jax.ShapeDtypeStruct((16, 512), F32)
    out = pl.pallas_call(
        functools.partial(kernel, ns, ng),
        out_shape=jax.ShapeDtypeStruct((2, 16, 512), F32),
        in_specs=[vmem] * 11,
        out_specs=vmem,
        scratch_shapes=[
            pltpu.VMEM((rows, 128), jnp.int32),
            pltpu.VMEM((rows, 128), jnp.int32),
            pltpu.VMEM((rows, 128), jnp.int32),
            pltpu.VMEM((rows // 8, 128, 1024), BF16),
            pltpu.VMEM((64, 128), F32),
            pltpu.VMEM((rows, 128), F32),
            pltpu.VMEM((64, 128), F32),
            pltpu.VMEM((8, 16, 128), F32),
            pltpu.VMEM((4, ns, 1, 128), F32),
            pltpu.VMEM((4, ns, 1, 128), F32),
            pltpu.VMEM((4, 2, FACE, 128), F32),
            pltpu.VMEM((4, 2, FACE, 128), F32),
            pltpu.VMEM((4, 1, 128), F32),
            pltpu.VMEM((4, ns, 1, 128), F32),
            pltpu.VMEM((2, 1, 128), F32),
            pltpu.VMEM((2, ng, 1, 128), F32),
            pltpu.VMEM((ns, 1, 256), F32),
            pltpu.VMEM((ns, 1, 256), F32),
            pltpu.VMEM((ns, 1, 256), jnp.int32),
            pltpu.VMEM((ns, 1, 256), jnp.int32),
            pltpu.VMEM((8, 128), jnp.int32),
            pltpu.VMEM((8, ns, 128), F32),
            pltpu.SemaphoreType.DMA((20,)),
            pltpu.SemaphoreType.DMA((20,)),
        ],
        compiler_params=pltpu.CompilerParams(collective_id=0, has_side_effects=True),
    )(*args, mats, corner)
    return out[0], out[1]


def solution(mesh):
    in_specs = (
        P(("grp", "sub"), None),
        P(("grp", "sub"), None),
        P(("grp", "sub"), None),
        P(("grp", "sub"), None),
        P(None, ("grp", "sub")),
        P(("grp", "sub"), None, None),
        P(None, ("grp", "sub")),
        P(None, ("grp", "sub")),
        P("grp", None, None),
    )
    out_specs = (P(("grp", "sub"), None), P(("grp", "sub"), None))
    return jax.shard_map(
        functools.partial(body, mesh.shape["sub"], mesh.shape["grp"]),
        mesh=mesh,
        in_specs=in_specs,
        out_specs=out_specs,
        check_vma=False,
    )
```

```python
import functools

import jax
import jax.numpy as jnp
import numpy as np
from jax import lax
from jax.experimental import pallas as pl
from jax.experimental.pallas import tpu as pltpu
from jax.sharding import PartitionSpec as P

MESH = pl.DeviceIdType.MESH
F32 = jnp.float32
BF16 = jnp.bfloat16
PAIR = 8
FACE = 4


def tables():
    order_index = np.arange(8)
    colloc = np.cos(np.pi * order_index / 7.0)
    end_weights = (
        np.where((order_index == 0) | (order_index == 7), 2.0, 1.0) * (-1.0) ** order_index
    )
    spacing = colloc[:, None] - colloc[None, :] + np.eye(8)
    raw_matrix = np.outer(end_weights, 1.0 / end_weights) / spacing
    off_part = raw_matrix * (1.0 - np.eye(8))
    derivative = 0.25 * (off_part - np.eye(8) * off_part.sum(axis=1)[:, None])
    derivative = derivative.astype(np.float32).astype(np.float64)
    eye2, eye8, eye16 = np.eye(2), np.eye(8), np.eye(16)

    def rows_matrix(mat):
        def part(out_low, in_low):
            return np.kron(mat[out_low::2, in_low::2], eye16)

        return np.block([[part(0, 0), part(0, 1)], [part(1, 1), part(1, 0)]])

    along_second = np.kron(eye2, np.kron(derivative, eye8)).T
    along_third = np.kron(eye16, derivative).T
    stack = [
        along_second,
        along_third,
        along_second.T,
        along_third.T,
        rows_matrix(derivative),
        rows_matrix(derivative.T),
    ]
    high = [np.asarray(m, np.float32).astype(jnp.bfloat16) for m in stack]
    low = [
        (np.asarray(m, np.float32) - h.astype(np.float32)).astype(jnp.bfloat16)
        for m, h in zip(stack, high)
    ]
    mats = np.stack(high + low)
    point_index = np.arange(512)
    corner_index = np.arange(8)
    sign_first = 1.0 - 2.0 * (corner_index >> 2 & 1)
    sign_second = 1.0 - 2.0 * (corner_index >> 1 & 1)
    sign_third = 1.0 - 2.0 * (corner_index & 1)
    node_first = colloc[point_index // 64][:, None]
    node_second = colloc[point_index // 8 % 8][:, None]
    node_third = colloc[point_index % 8][:, None]
    corner = (
        0.5
        * (1.0 + sign_first[None, :] * node_first)
        * (0.5 * (1.0 + sign_second[None, :] * node_second))
        * (0.5 * (1.0 + sign_third[None, :] * node_third))
    )
    factors = np.zeros((8, 512))
    factors[0, :8] = 0.5 * (1.0 + colloc)
    factors[0, 8:16] = 0.5 * (1.0 - colloc)
    return jnp.asarray(mats), jnp.asarray(np.concatenate([corner.T, factors]), F32)


def kernel(
    ns,
    ng,
    right_ref,
    metric_ref,
    helm_ref,
    jac_ref,
    pair_ref,
    slots_ref,
    face_ref,
    map_ref,
    cinv_ref,
    mats_ref,
    corner_ref,
    out_ref,
    idx,
    hi_ref,
    lo_ref,
    ohlo,
    x_ref,
    val_ref,
    cscr,
    mcol,
    send_s,
    recv_s,
    send_f,
    recv_f,
    send_r,
    recv_r,
    send_b,
    recv_b,
    send_h,
    recv_h,
    send_t,
    recv_t,
    map_scr,
    phi,
    send_sem,
    recv_sem,
):
    g = lax.axis_index("grp")
    s = lax.axis_index("sub")
    nxt, prv = lax.rem(g + 1, ng), lax.rem(g + ng - 1, ng)
    rows = 2 * PAIR + ns + 2 * FACE
    tiles = rows // 8
    at_pair = ns + 2 * FACE

    recv_s[...] = jnp.zeros_like(recv_s)
    recv_h[...] = jnp.zeros_like(recv_h)
    recv_t[...] = jnp.zeros_like(recv_t)

    def far_first(step, count):
        return count // 2 + (1 - 2 * lax.rem(step, 2)) * lax.div(step + 1, 2)

    def sub_peer(step):
        row = lax.div(s, 4) + far_first(lax.div(step, 4), ns // 4)
        column = lax.rem(s, 4) + far_first(lax.rem(step, 4), 4)
        return lax.rem(row, ns // 4) * 4 + lax.rem(column, 4)

    def grp_peer(step):
        return lax.rem(g + far_first(step, ng), ng)

    barrier = pltpu.get_barrier_semaphore()

    def greet_sub(k, carry):
        pl.semaphore_signal(
            barrier, inc=1, device_id={"sub": sub_peer(k)}, device_id_type=MESH
        )
        return carry

    def greet_grp(k, carry):
        pl.semaphore_signal(
            barrier, inc=1, device_id={"grp": grp_peer(k)}, device_id_type=MESH
        )
        return carry

    lax.fori_loop(0, ns - 1, greet_sub, 0, unroll=True)
    lax.fori_loop(0, ng - 1, greet_grp, 0, unroll=True)

    def cube(ref, base=0):
        return jnp.concatenate(
            [ref[:, base + 128 * k : base + 128 * (k + 1)] for k in range(4)], axis=0
        )

    def total(x):
        return jnp.sum(jnp.sum(x, axis=0, keepdims=True), axis=1, keepdims=True)

    lane = lax.broadcasted_iota(jnp.int32, (1, 128), 1)

    def pick(row, k):
        return jnp.sum(jnp.where(lane == k, row, 0.0), axis=1, keepdims=True)

    def put(k, value):
        return jnp.where(lane == k, value, 0.0)

    eye_16 = lax.broadcasted_iota(jnp.int32, (16, 16), 0) == lax.broadcasted_iota(
        jnp.int32, (16, 16), 1
    )
    lane_16 = lax.broadcasted_iota(jnp.int32, (16, 128), 1).astype(F32)
    for q in range(8):
        column = jnp.sum(
            jnp.where(eye_16, map_ref[q : q + 1, :].astype(F32), 0.0), axis=1, keepdims=True
        )
        mcol[q] = jnp.where(lane_16 == column, 1.0, 0.0)
    cscr[...] = jnp.zeros_like(cscr)
    cscr[:, :64] = cinv_ref[0]

    def restrict(x):
        row = jnp.zeros((1, 128), F32)
        for q in range(8):
            acc = x[:16] * corner_ref[q : q + 1, :128]
            for k in range(1, 4):
                acc += x[16 * k : 16 * (k + 1)] * corner_ref[q : q + 1, 128 * k : 128 * (k + 1)]
            vertex = jnp.sum(acc, axis=1, keepdims=True)
            row += jnp.sum(vertex * mcol[q], axis=0, keepdims=True)
        return row

    eye_64 = lax.broadcasted_iota(jnp.int32, (64, 128), 0) == lax.broadcasted_iota(
        jnp.int32, (64, 128), 1
    )

    def solve(coarse):
        column = jnp.sum(jnp.where(eye_64, coarse, 0.0), axis=1, keepdims=True)
        return jnp.sum(cscr[...] * column, axis=0, keepdims=True)

    def prolong(solved):
        blocks = [jnp.zeros((16, 128), F32) for _ in range(4)]
        for q in range(8):
            at_vertex = jnp.sum(mcol[q] * solved, axis=1, keepdims=True)
            for k in range(4):
                blocks[k] += at_vertex * corner_ref[q : q + 1, 128 * k : 128 * (k + 1)]
        return jnp.concatenate(blocks, axis=0)

    def copy_sub(src, dst, sem, peer):
        return pltpu.make_async_remote_copy(
            src_ref=src,
            dst_ref=dst,
            send_sem=send_sem.at[sem],
            recv_sem=recv_sem.at[sem],
            device_id={"sub": peer},
            device_id_type=MESH,
        )

    def copy_grp(src, dst, sem, peer):
        return pltpu.make_async_remote_copy(
            src_ref=src,
            dst_ref=dst,
            send_sem=send_sem.at[sem],
            recv_sem=recv_sem.at[sem],
            device_id={"grp": peer},
            device_id_type=MESH,
        )

    def wait_bytes(ref, sem):
        pltpu.make_async_copy(ref, ref, sem).wait()

    def sum_sub_start(phase, row):
        send_r[phase] = row
        recv_r[phase, s] = row

        def go(k, carry):
            peer = sub_peer(k)
            copy_sub(send_r.at[phase], recv_r.at[phase, s], 12 + phase, peer).start()
            return carry

        lax.fori_loop(0, ns - 1, go, 0, unroll=True)

    def sum_sub(phase):
        wait_bytes(recv_r.at[phase, pl.ds(0, ns - 1)], recv_sem.at[12 + phase])
        return jnp.sum(recv_r[phase], axis=0)

    def sum_grp_start(phase, row):
        send_b[phase] = row
        recv_b[phase, g] = row

        def go(k, carry):
            peer = grp_peer(k)
            copy_grp(send_b.at[phase], recv_b.at[phase, g], 16 + phase, peer).start()
            return carry

        lax.fori_loop(0, ng - 1, go, 0, unroll=True)

    def sum_grp(phase):
        wait_bytes(recv_b.at[phase, pl.ds(0, ng - 1)], recv_sem.at[16 + phase])
        return jnp.sum(recv_b[phase], axis=0)

    residual = cube(right_ref)
    partial_coarse = restrict(residual)

    idx[:ns, :] = slots_ref[0]
    for k in range(2):
        for m in range(FACE):
            at = ns + FACE * k + m
            idx[at : at + 1, :] = face_ref[k : k + 1, 128 * m : 128 * (m + 1)]
        for m in range(PAIR):
            at = at_pair + PAIR * k + m
            idx[at : at + 1, :] = pair_ref[k : k + 1, 128 * m : 128 * (m + 1)]
    points = idx[...]
    row_of = ((points >> 7) & 3) * 16 + (points >> 9)
    hi_ref[...] = jnp.where(points >= 8192, 1024, row_of)
    lo_ref[...] = points & 127

    def gather(first, last):
        high = hi_ref[first:last, :]
        low = lo_ref[first:last, :]

        def step(t, acc):
            block = x_ref[pl.ds(pl.multiple_of(t * 8, 8), 8), :]
            for r in range(8):
                row = jnp.broadcast_to(block[r : r + 1], (last - first, 128))
                got = jnp.take_along_axis(row, low, axis=1, mode="promise_in_bounds")
                acc = jnp.where(high == t * 8 + r, got, acc)
            return acc

        return lax.fori_loop(
            0, 8, step, jnp.zeros((last - first, 128), F32), unroll=True
        )

    def look(table, at):
        return jnp.take_along_axis(table, at, axis=1, mode="promise_in_bounds")

    map_scr[...] = jnp.zeros_like(map_scr)
    map_scr[:, :16] = map_ref[...]
    lane_8 = lax.broadcasted_iota(jnp.int32, (8, 128), 1)
    corner_row = lax.broadcasted_iota(jnp.int32, (8, 128), 0) == lane_8 >> 4
    spread = look(map_scr[...], lane_8 & 15).astype(F32)
    map_row = jnp.sum(jnp.where(corner_row, spread, 0.0), axis=0, keepdims=True)
    x_ref[...] = cube(jac_ref) * residual
    send_h[:, :, :128] = jnp.broadcast_to(partial_coarse.reshape(1, 1, 128), (ns, 1, 128))
    send_h[:, :, 128:] = gather(0, ns).reshape(ns, 1, 128)
    send_t[:, :, :128] = jnp.broadcast_to(
        map_row.astype(jnp.int32).reshape(1, 1, 128), (ns, 1, 128)
    )
    send_t[:, :, 128:] = points[:ns].reshape(ns, 1, 128)
    recv_h[s, :, :128] = partial_coarse

    pl.semaphore_wait(barrier, ns + ng - 2)

    def hello(k, carry):
        peer = sub_peer(k)
        copy_sub(send_h.at[peer], recv_h.at[s], 18, peer).start()
        return carry

    def hello_tables(k, carry):
        peer = sub_peer(k)
        copy_sub(send_t.at[peer], recv_t.at[s], 19, peer).start()
        return carry

    lax.fori_loop(0, ns - 1, hello, 0, unroll=True)
    lax.fori_loop(0, ns - 1, hello_tables, 0, unroll=True)

    sub_128 = lax.broadcasted_iota(jnp.int32, (128, 128), 0)
    sub_64 = lax.broadcasted_iota(jnp.int32, (64, 128), 0)

    def build(t, carry):
        low = lo_ref[pl.ds(pl.multiple_of(t * 8, 8), 8), :]
        ohlo[t] = jnp.concatenate(
            [jnp.where(sub_128 == low[r : r + 1], 1.0, 0.0).astype(BF16) for r in range(8)],
            axis=1,
        )
        return carry

    lax.fori_loop(0, tiles, build, 0, unroll=True)

    def scatter(first, last, acc):
        def step(t, acc):
            at = pl.ds(pl.multiple_of(t * 8, 8), 8)
            high = hi_ref[at, :]
            value = val_ref[at, :]
            upper = value.astype(BF16).astype(F32)
            lower = value - upper
            parts = []
            for r in range(8):
                hit = sub_64 == high[r : r + 1]
                parts.append(
                    jnp.concatenate(
                        [
                            jnp.where(hit, upper[r : r + 1], 0.0),
                            jnp.where(hit, lower[r : r + 1], 0.0),
                        ],
                        axis=0,
                    ).astype(BF16)
                )
            left = jnp.concatenate(parts, axis=1)
            return acc + lax.dot_general(
                left, ohlo[t], (((1,), (1,)), ((), ())), preferred_element_type=F32
            )

        return lax.fori_loop(first, last, step, acc, unroll=True)

    def send_slots(phase):
        send_s[phase] = gather(0, ns).reshape(ns, 1, 128)

        def go(k, carry):
            peer = sub_peer(k)
            copy_sub(send_s.at[phase, peer], recv_s.at[phase, s], phase, peer).start()
            return carry

        lax.fori_loop(0, ns - 1, go, 0, unroll=True)

    def send_faces(phase):
        got = gather(ns, at_pair)
        send_f[phase, 0] = got[:FACE]
        send_f[phase, 1] = got[FACE:]
        down = copy_grp(send_f.at[phase, 0], recv_f.at[phase, 1], 4 + phase, prv)
        up = copy_grp(send_f.at[phase, 1], recv_f.at[phase, 0], 8 + phase, nxt)
        down.start()
        up.start()
        return down, up

    def add_pairs():
        got = gather(at_pair, rows)
        val_ref[at_pair : at_pair + PAIR, :] = got[PAIR:]
        val_ref[at_pair + PAIR :, :] = got[:PAIR]
        return scatter(at_pair // 8, tiles, jnp.zeros((128, 128), F32))

    def add_faces(phase, copies, acc):
        for copy in copies:
            copy.wait_recv()
        val_ref[ns : ns + FACE, :] = jnp.where(g == 0, 0.0, recv_f[phase, 0])
        val_ref[ns + FACE : at_pair, :] = jnp.where(g == ng - 1, 0.0, recv_f[phase, 1])
        return scatter(ns // 8, at_pair // 8, acc)

    def wait_slots(phase):
        wait_bytes(recv_s.at[phase, pl.ds(0, ns - 1)], recv_sem.at[phase])
        return recv_s[phase].reshape(ns, 128)

    def add_slots(value, acc):
        val_ref[:ns, :] = value
        return scatter(0, ns // 8, acc)

    def assemble(phase, x, meanwhile=lambda: None, before_slots=lambda: None):
        x_ref[...] = x
        send_slots(phase)
        copies = send_faces(phase)
        meanwhile()
        acc = add_faces(phase, copies, add_pairs())
        before_slots()
        acc = add_slots(wait_slots(phase), acc)
        return x + acc[:64] + acc[64:]

    def assemble_known(phase, x, slot_values):
        x_ref[...] = x
        copies = send_faces(phase)
        acc = add_pairs()
        acc = add_slots(slot_values(), acc)
        acc = add_faces(phase, copies, acc)
        return x + acc[:64] + acc[64:]

    def peer_points():
        return recv_t[:, :, 128:].reshape(ns, 128)

    def corner_functions():
        point = peer_points()
        table = jnp.broadcast_to(corner_ref[8:9, :128], (ns, 128))
        nodes = [(point >> 6) & 7, (point >> 3) & 7, point & 7]
        near = [[look(table, node + 8 * bit) for bit in range(2)] for node in nodes]
        for q in range(8):
            phi[q] = near[0][q >> 2 & 1] * near[1][q >> 1 & 1] * near[2][q & 1]

    def coarse_at_peers(solved):
        corners = look(jnp.broadcast_to(solved, (ns, 128)), recv_t[:, :, :128].reshape(ns, 128))
        element = (peer_points() >> 9) & 15
        out = jnp.zeros((ns, 128), F32)
        for q in range(8):
            out += phi[q] * look(corners, element + 16 * q)
        return out

    def split(x):
        upper = x.astype(BF16)
        return upper, (x - upper.astype(F32)).astype(BF16)

    def dot(a, b):
        return jnp.dot(a, b, preferred_element_type=F32)

    def dot_right(x, k):
        upper, lower = split(x)
        both = dot(jnp.concatenate([upper, lower], axis=0), mats_ref[k])
        return both[:64] + both[64:] + dot(upper, mats_ref[k + 6])

    left_half = lax.broadcasted_iota(jnp.int32, (64, 128), 1) < 64

    def dot_rows(x, k):
        upper, lower = split(jnp.concatenate([x, pltpu.roll(x, 64, 1)], axis=0))
        both = dot(mats_ref[k], jnp.concatenate([upper, lower], axis=1))
        out = both[:, :128] + both[:, 128:] + dot(mats_ref[k + 6], upper)
        return jnp.where(left_half, out[:64], out[64:])

    def stiffness(x):
        flux_first = cube(metric_ref, 0) * dot_rows(x, 4)
        flux_second = cube(metric_ref, 512) * dot_right(x, 0)
        flux_third = cube(metric_ref, 1024) * dot_right(x, 1)
        return dot_rows(flux_first, 5) + dot_right(flux_second, 2) + dot_right(flux_third, 3)

    right = residual
    part = cube(jac_ref) * right
    wait_bytes(recv_h.at[pl.ds(0, ns - 1)], recv_sem.at[18])
    solved = solve(jnp.sum(recv_h[:, :, :128], axis=0))
    first = part + prolong(solved)

    def first_slots():
        wait_bytes(recv_t.at[pl.ds(0, ns - 1)], recv_sem.at[19])
        corner_functions()
        return recv_h[:, :, 128:].reshape(ns, 128) + coarse_at_peers(solved)

    summed = assemble_known(0, first, first_slots)
    inner = stiffness(summed)
    mass = cube(helm_ref) * first

    def first_sums():
        row = put(0, total(right * first)) + put(1, total(summed * inner + first * mass))
        sum_sub_start(1, row)

    image = assemble(1, inner, first_sums)
    image += mass
    sum_sub_start(2, restrict(image))
    part = cube(jac_ref) * image
    x_ref[...] = part
    send_slots(2)
    sum_grp_start(0, sum_sub(1))
    solved_second = solve(sum_sub(2))
    second = part + prolong(solved_second)

    def second_slots():
        known = coarse_at_peers(solved_second)
        return wait_slots(2) + known

    summed_second = assemble_known(2, second, second_slots)
    inner_second = stiffness(summed_second)
    sums = sum_grp(0)
    rz_first, curved = pick(sums, 0), pick(sums, 1)
    alpha = rz_first / curved
    residual = right - alpha * image
    smoothed = first - alpha * second
    row = (
        put(0, total(residual * smoothed))
        + put(1, total(smoothed * image))
        + put(
            2,
            total(
                (summed - alpha * summed_second) * (inner - alpha * inner_second)
                + smoothed * (cube(helm_ref) * smoothed)
            ),
        )
    )
    sum_sub_start(3, row)

    def last_sums():
        sum_grp_start(1, sum_sub(3))

    image_second = assemble(3, inner_second, before_slots=last_sums)
    image_second += cube(helm_ref) * second
    sums = sum_grp(1)
    rz_second = pick(sums, 0)
    beta = rz_second / rz_first
    curve = pick(sums, 2) + 2.0 * beta * pick(sums, 1) + beta * beta * curved
    alpha_last = rz_second / curve
    solved = alpha * first + alpha_last * (smoothed + beta * first)
    residual = residual - alpha_last * (image - alpha * image_second + beta * image)
    for k in range(4):
        out_ref[0, :, 128 * k : 128 * (k + 1)] = solved[16 * k : 16 * (k + 1)]
        out_ref[1, :, 128 * k : 128 * (k + 1)] = residual[16 * k : 16 * (k + 1)]

    for phase in range(1, 4):
        wait_bytes(send_s.at[phase, pl.ds(0, ns - 1)], send_sem.at[phase])
    for phase in range(4):
        wait_bytes(send_f.at[phase, 0], send_sem.at[4 + phase])
        wait_bytes(send_f.at[phase, 1], send_sem.at[8 + phase])
    wait_bytes(send_h.at[pl.ds(0, ns - 1)], send_sem.at[18])
    wait_bytes(send_t.at[pl.ds(0, ns - 1)], send_sem.at[19])
    for phase in range(1, 4):
        wait_bytes(recv_r.at[phase, pl.ds(0, ns - 1)], send_sem.at[12 + phase])
    for phase in range(2):
        wait_bytes(recv_b.at[phase, pl.ds(0, ng - 1)], send_sem.at[16 + phase])


def body(ns, ng, *args):
    mats, corner = tables()
    rows = 2 * PAIR + ns + 2 * FACE
    vmem = pl.BlockSpec(memory_space=pltpu.VMEM)
    shape = jax.ShapeDtypeStruct((16, 512), F32)
    out = pl.pallas_call(
        functools.partial(kernel, ns, ng),
        out_shape=jax.ShapeDtypeStruct((2, 16, 512), F32),
        in_specs=[vmem] * 11,
        out_specs=vmem,
        scratch_shapes=[
            pltpu.VMEM((rows, 128), jnp.int32),
            pltpu.VMEM((rows, 128), jnp.int32),
            pltpu.VMEM((rows, 128), jnp.int32),
            pltpu.VMEM((rows // 8, 128, 1024), BF16),
            pltpu.VMEM((64, 128), F32),
            pltpu.VMEM((rows, 128), F32),
            pltpu.VMEM((64, 128), F32),
            pltpu.VMEM((8, 16, 128), F32),
            pltpu.VMEM((4, ns, 1, 128), F32),
            pltpu.VMEM((4, ns, 1, 128), F32),
            pltpu.VMEM((4, 2, FACE, 128), F32),
            pltpu.VMEM((4, 2, FACE, 128), F32),
            pltpu.VMEM((4, 1, 128), F32),
            pltpu.VMEM((4, ns, 1, 128), F32),
            pltpu.VMEM((2, 1, 128), F32),
            pltpu.VMEM((2, ng, 1, 128), F32),
            pltpu.VMEM((ns, 1, 256), F32),
            pltpu.VMEM((ns, 1, 256), F32),
            pltpu.VMEM((ns, 1, 256), jnp.int32),
            pltpu.VMEM((ns, 1, 256), jnp.int32),
            pltpu.VMEM((8, 128), jnp.int32),
            pltpu.VMEM((8, ns, 128), F32),
            pltpu.SemaphoreType.DMA((20,)),
            pltpu.SemaphoreType.DMA((20,)),
        ],
        compiler_params=pltpu.CompilerParams(collective_id=0, has_side_effects=True),
    )(*args, mats, corner)
    return out[0], out[1]


def solution(mesh):
    in_specs = (
        P(("grp", "sub"), None),
        P(("grp", "sub"), None),
        P(("grp", "sub"), None),
        P(("grp", "sub"), None),
        P(None, ("grp", "sub")),
        P(("grp", "sub"), None, None),
        P(None, ("grp", "sub")),
        P(None, ("grp", "sub")),
        P("grp", None, None),
    )
    out_specs = (P(("grp", "sub"), None), P(("grp", "sub"), None))
    return jax.shard_map(
        functools.partial(body, mesh.shape["sub"], mesh.shape["grp"]),
        mesh=mesh,
        in_specs=in_specs,
        out_specs=out_specs,
        check_vma=False,
    )
```
